256 devices in a mesh: brick: 32 (over z, x), scene: 8 (over y, core).
Axes of the slice: x: 4, y: 4, z: 8, core: 2. Of those that a mesh axis runs over, the one named last changes fastest.
Arguments:
- features: float32 [8, 128, 64, 512], P('scene', 'brick'), may hold values from -6 to 6
- cotangent: float32 [8, 128, 64, 512], P('scene', 'brick'), may hold values from -6 to 6
- first_kernel: float32 [27, 64, 64], replicated, may hold values from -0.15625 to 0.15625
- second_kernel: float32 [27, 64, 64], replicated, may hold values from -0.15625 to 0.15625
- counts: int32 [32], P('brick'), may hold values from 1 to 4, as said below
- neighbours: int32 [128, 26], P('brick'), may hold values from -1 to 127, as said below
Outputs:
- out_features: float32 [8, 128, 64, 512], P('scene', 'brick')
- feature_grad: float32 [8, 128, 64, 512], P('scene', 'brick')
- first_grad: float32 [27, 64, 64], replicated
- second_grad: float32 [27, 64, 64], replicated
The draws below stay inside these ranges and needn't reach their ends.
Inputs may be any that keep to these rules, and one draw needn't show every extreme that they name: Index d of brick owns counts[d] bricks in its slots 0 to counts[d] - 1; some index owns 4. `neighbours`: entries name occupied slots; the relation is symmetric (if slot t is the neighbour of s in direction (a, b, c), s is the neighbour of t in (-a, -b, -c)); unoccupied slots have only -1. A neighbour in a direction with c = 0 is owned by the same index of brick, with c = 1 by the same or the next index, with c = -1 by the same or the previous index.
All inputs are finite; a program needn't handle non-finite values.
Results may differ from the reference program's by a relative error of at most 0.0057.
Values may be sent and summed in bfloat16 or wider, within the bound.
No kernel may reach another device: no remote copies, remote signals or barrier semaphores. Data moves between devices by JAX's collectives and lax.ppermute only.
A program may use at most 128 MiB of HBM per device.

```python
import jax
import jax.numpy as jnp
from jax import lax

C = 64
E = 8
ZL = 1
V = 512
CAP = 4
SLOTS = 128
SCENES = 8
N_BRICK = 32


offsets = [(a, b, c) for a in (-1, 0, 1) for b in (-1, 0, 1) for c in (-1, 0, 1)]


directions = [item for item in offsets if item != (0, 0, 0)]


def geometry(key):
    base_key = jax.random.fold_in(key, 1234)
    key_level, key_roll = jax.random.split(base_key, 2)
    density = jax.random.randint(key_level, (N_BRICK, 1), 1, 5)
    rolled = jax.random.randint(key_roll, (N_BRICK, CAP), 0, 4)
    chosen = N_BRICK - 1
    row_ids = jnp.arange(N_BRICK, dtype=jnp.int32)[:, None]
    places = jnp.arange(CAP, dtype=jnp.int32)[None, :]
    active = (rolled < density) | (row_ids == chosen) | (places == 0)
    counts = jnp.sum(active.astype(jnp.int32), axis=1)
    scores = jnp.where(active, places, places + CAP)
    slot_order = jnp.argsort(scores, axis=1, stable=True).astype(jnp.int32)
    slot_rank = jnp.argsort(slot_order, axis=1, stable=True).astype(jnp.int32)
    slot_of = jnp.where(active, row_ids * CAP + slot_rank, -1)
    pos_x = slot_order % 2
    pos_y = slot_order // 2 % 2
    pos_z = row_ids * ZL + slot_order // 4
    filled = places < counts[:, None]
    layers = N_BRICK * ZL
    columns = []
    for a, b, c in directions:
        near_x = pos_x + a
        near_y = pos_y + b
        near_z = pos_z + c
        inside = (near_x >= 0) & (near_x < 2) & (near_y >= 0) & (near_y < 2) & (near_z >= 0) & (near_z < layers)
        clipped_z = jnp.clip(near_z, 0, layers - 1)
        owner_row = clipped_z // ZL
        near_place = jnp.clip(near_x, 0, 1) + 2 * jnp.clip(near_y, 0, 1) + 4 * (clipped_z % ZL)
        target = slot_of[owner_row, near_place]
        columns.append(jnp.where(inside & filled, target, -1))
    neighbours = jnp.stack(columns, axis=-1).reshape(N_BRICK * CAP, 26).astype(jnp.int32)
    return (counts.astype(jnp.int32), neighbours)


def draw_counts(key, part):
    return geometry(key)[0]


def draw_neighbours(key, part):
    return geometry(key)[1]


def shard_levels(rng, dims, cuts, smallest, high):
    level = 1.0
    for dim, blocks in cuts:
        heights = jax.random.uniform(jax.random.fold_in(jax.random.fold_in(rng, 6), dim), (blocks,), jnp.float32, smallest / len(cuts), high / len(cuts))
        level = level * jnp.repeat(jnp.exp(heights), dims[dim] // blocks).reshape((-1,) + (1,) * (len(dims) - 1 - dim))
    return level


def centred(key, shape, scale, bound, cuts=(), kind=jnp.bfloat16):
    level = shard_levels(key, shape, cuts, -0.22, 0.18) if cuts else 1.0
    entries = jax.random.normal(key, shape, jnp.float32) * scale * level
    return jnp.minimum(jnp.maximum(entries, -bound), bound).astype(kind)


def setup_inputs(seed: int = 0) -> dict:
    key_list = jax.random.split(jax.random.key(seed), 7)
    features = centred(key_list[0], (SCENES, SLOTS, C, V), 1.0, 6.0, ((0, 8), (1, 32)), jnp.float32)
    cotangent = centred(key_list[1], (SCENES, SLOTS, C, V), 1.0, 6.0, ((0, 8), (1, 32)), jnp.float32)
    first_kernel = centred(key_list[2], (27, C, C), (27 * C) ** -0.5, 0.15625, (), jnp.float32)
    second_kernel = centred(key_list[3], (27, C, C), (27 * C) ** -0.5, 0.15625, (), jnp.float32)
    counts = draw_counts(jax.random.fold_in(key_list[6], 71), 0)
    neighbours = draw_neighbours(jax.random.fold_in(key_list[6], 71), 0)
    return {"features": features, "cotangent": cotangent, "first_kernel": first_kernel, "second_kernel": second_kernel, "counts": counts, "neighbours": neighbours}


offsets = [(a, b, c) for a in (-1, 0, 1) for b in (-1, 0, 1) for c in (-1, 0, 1)]
directions = [item for item in offsets if item != (0, 0, 0)]

def source_range(offset, edge_cells):
    if offset < 0:
        return (edge_cells - 1, edge_cells)
    if offset == 0:
        return (0, edge_cells)
    return (0, 1)

def target_range(offset, edge_cells):
    if offset < 0:
        return (0, 1)
    if offset == 0:
        return (1, edge_cells + 1)
    return (edge_cells + 1, edge_cells + 2)

def assemble(center, sources, indices, present, edge_cells):
    slot_count, chans = (center.shape[0], center.shape[1])
    padded = jnp.zeros((slot_count, chans, edge_cells + 2, edge_cells + 2, edge_cells + 2), center.dtype)
    padded = padded.at[:, :, 1:edge_cells + 1, 1:edge_cells + 1, 1:edge_cells + 1].set(center)
    for number, (a, b, c) in enumerate(directions):
        source = sources[c + 1]
        range_i = source_range(a, edge_cells)
        range_j = source_range(b, edge_cells)
        depth_range = source_range(c, edge_cells) if c == 0 else (0, 1)
        slab_part = source[:, :, range_i[0]:range_i[1], range_j[0]:range_j[1], depth_range[0]:depth_range[1]]
        last_row = source.shape[0] - 1
        chosen_rows = jnp.clip(indices[c + 1][:, number], 0, last_row).astype(jnp.int32)
        picked = jnp.take(slab_part, chosen_rows, axis=0)
        picked = jnp.where(present[:, number][:, None, None, None, None], picked, jnp.zeros_like(picked))
        target_i = target_range(a, edge_cells)
        target_j = target_range(b, edge_cells)
        target_l = target_range(c, edge_cells)
        padded = padded.at[:, :, target_i[0]:target_i[1], target_j[0]:target_j[1], target_l[0]:target_l[1]].set(picked)
    return padded

def window_of(padded, number):
    a, b, c = offsets[number]
    slot_count, chans = (padded.shape[0], padded.shape[1])
    part = padded[:, :, 1 + a:1 + a + E, 1 + b:1 + b + E, 1 + c:1 + c + E]
    return part.reshape(slot_count, chans, E * E * E).astype(jnp.float32)

def apply_kernel(padded, weight, transpose):
    weight_f = weight.astype(jnp.bfloat16).astype(jnp.float32)
    accum = None
    for number in range(27):
        window = window_of(padded, number)
        if transpose:
            term = jnp.einsum('io,sop->sip', weight_f[26 - number], window, precision=lax.Precision.HIGHEST)
        else:
            term = jnp.einsum('io,sip->sop', weight_f[number], window, precision=lax.Precision.HIGHEST)
        accum = term if accum is None else accum + term
    return accum

def kernel_terms(padded, errors):
    errors_f = errors.astype(jnp.bfloat16).astype(jnp.float32)
    return jnp.stack([jnp.einsum('sip,sop->io', window_of(padded, number), errors_f, precision=lax.Precision.HIGHEST) for number in range(27)])

def slope(values):
    sig = jax.nn.sigmoid(values)
    return sig * (1.0 + values * (1.0 - sig))

def reference(features, cotangent, first_kernel, second_kernel, counts, neighbours):
    slot_ids = jnp.arange(SLOTS, dtype=jnp.int32)
    occupied = (slot_ids % CAP < counts[slot_ids // CAP]).astype(jnp.float32)[:, None, None]
    present = neighbours >= 0
    indices = (neighbours, neighbours, neighbours)

    def padded_of(values):
        cubes = values.astype(jnp.bfloat16).reshape(SLOTS, C, E, E, E)
        sources = (cubes[..., E - 1:E], cubes, cubes[..., 0:1])
        return assemble(cubes, sources, indices, present, E)

    def one_scene(pair):
        inputs = pair[0] * occupied
        upstream = pair[1] * occupied
        padded_in = padded_of(inputs)
        first_pre = apply_kernel(padded_in, first_kernel, False)
        hidden = inputs + jax.nn.silu(first_pre)
        padded_hidden = padded_of(hidden)
        second_pre = apply_kernel(padded_hidden, second_kernel, False)
        outputs = hidden + jax.nn.silu(second_pre)
        second_err = upstream * slope(second_pre)
        hidden_grad = upstream + apply_kernel(padded_of(second_err), second_kernel, True)
        second_local = kernel_terms(padded_hidden, second_err)
        first_err = hidden_grad * slope(first_pre)
        input_grad = hidden_grad + apply_kernel(padded_of(first_err), first_kernel, True)
        first_local = kernel_terms(padded_in, first_err)
        return (outputs, input_grad, first_local, second_local)
    outputs, input_grad, first_all, second_all = lax.map(one_scene, (features, cotangent))
    scale = 1.0 / jnp.sqrt(jnp.float32(SCENES * SLOTS * V))
    return (outputs, input_grad, lax.optimization_barrier(jnp.sum(first_all, axis=0)) * scale, lax.optimization_barrier(jnp.sum(second_all, axis=0)) * scale)
```

```python
import jax
import jax.numpy as jnp
from jax import lax
from jax.experimental import pallas as pl
from jax.experimental.pallas import tpu as pltpu
from jax.sharding import PartitionSpec as P

E = 8
C = 64
CAP = 4
f32 = jnp.float32
bf16 = jnp.bfloat16
offsets = [(a, b, c) for a in (-1, 0, 1) for b in (-1, 0, 1) for c in (-1, 0, 1)]
directions = [item for item in offsets if item != (0, 0, 0)]
number_of = {item: n for n, item in enumerate(directions)}

ROWS = CAP * 256
PLANE = CAP * 32
PACKED = 896


def row0(s, n, l):
    return s * 256 + (n // 2) * 128 + l * 16 + (n % 2) * 8


def flip(t):
    tt = t.T
    return jnp.concatenate([tt[:C], tt[C:]], axis=1)


def lane_low(shape):
    return lax.broadcasted_iota(jnp.int32, shape, 1) < C


def to_rows(x_ref, a_ref, tmp_ref, counts_ref):
    for s in range(CAP):
        occupied = jnp.where(s < counts_ref[0], 1.0, 0.0).astype(f32)
        for n in range(4):
            t = x_ref[0, s, :, n * 128 : (n + 1) * 128] * occupied
            tmp_ref[s * 4 + n] = flip(t)
            for l in range(E):
                a_ref[pl.ds(row0(s, n, l), 8), :] = tmp_ref[s * 4 + n, pl.ds(l, 8, stride=8), :]


def from_rows(a_ref, o_ref, tmp_ref):
    for s in range(CAP):
        for n in range(4):
            for l in range(E):
                tmp_ref[s * 4 + n, pl.ds(l, 8, stride=8), :] = a_ref[pl.ds(row0(s, n, l), 8), :]
            o_ref[0, s, :, n * 128 : (n + 1) * 128] = flip(tmp_ref[s * 4 + n])


def planes_out(a_ref, up_ref, down_ref):
    for s in range(CAP):
        for nh in range(2):
            base = s * 256 + nh * 128
            to = pl.ds(s * 32 + nh * 16, 16)
            up_ref[to, :] = a_ref[pl.ds(base + 7 * 16, 16), :].astype(bf16)
            down_ref[to, :] = a_ref[pl.ds(base, 16), :].astype(bf16)


def pre_kernel(counts_ref, x_ref, a_ref, up_ref, down_ref, tmp_ref):
    to_rows(x_ref, a_ref, tmp_ref, counts_ref)
    planes_out(a_ref, up_ref, down_ref)


def flat_weights(w_ref, o_ref, back):
    zero = jnp.zeros((C, C), f32)

    def block(a, b, c):
        k = 9 * (a + 1) + 3 * (b + 1) + (c + 1)
        return w_ref[26 - k].T if back else w_ref[k]

    for ci, c in enumerate((-1, 0, 1)):
        for bi, b in enumerate((-1, 0, 1)):
            low, mid, high = (block(a, b, c) for a in (-1, 0, 1))
            rows = ((mid, low), (high, mid), (zero, high), (low, zero))
            for r, (left, right) in enumerate(rows):
                joined = jnp.concatenate([left, right], axis=1).astype(bf16)
                o_ref[ci, pl.ds(bi * 256 + r * C, C), :] = joined


def prep_kernel(counts_ref, w1_ref, w2_ref, x_ref, f1_ref, f2_ref, b1_ref, b2_ref, u_ref, tmp_ref):
    flat_weights(w1_ref, f1_ref, False)
    flat_weights(w2_ref, f2_ref, False)
    flat_weights(w1_ref, b1_ref, True)
    flat_weights(w2_ref, b2_ref, True)
    to_rows(x_ref, u_ref, tmp_ref, counts_ref)


def build(a_ref, lo_ref, hi_ref, idx_ref, g_ref, pool_ref, x_ref):
    g_ref[pl.ds(0, ROWS), :] = a_ref[...]
    g_ref[pl.ds(ROWS, 256), :] = jnp.zeros((256, 128), f32)
    for side, (ref, layer) in enumerate(((lo_ref, 7), (hi_ref, 0))):
        for s in range(CAP):
            for nh in range(2):
                pool_ref[side, pl.ds(s * 32 + nh * 16, 16), :] = a_ref[
                    pl.ds(s * 256 + nh * 128 + layer * 16, 16), :
                ]
        pool_ref[side, pl.ds(PLANE, PLANE), :] = ref[...].astype(f32)
        pool_ref[side, pl.ds(2 * PLANE, 32), :] = jnp.zeros((32, 128), f32)
    row = lax.broadcasted_iota(jnp.int32, (8, 128), 0)
    low = lane_low((8, 128))

    def one_slot(s, carry):
        def tile(a, b, c, n, l):
            nh, nl = n // 2, n % 2
            if (a, b, c) == (0, 0, 0):
                base = s * 256
            else:
                base = idx_ref[s, number_of[a, b, c]]
            if c == 0:
                return g_ref[pl.ds(pl.multiple_of(base + (nh * 128 + l * 16 + nl * 8), 8), 8), :]
            side = 0 if c < 0 else 1
            return pool_ref[side, pl.ds(pl.multiple_of(base + (nh * 16 + nl * 8), 8), 8), :]

        def pair(b, c, n, l):
            full = tile(0, b, c, n, l)
            after = tile(0, b, c, n + 1, l) if n < 3 else tile(1, b, c, 0, l)
            before = tile(0, b, c, n - 1, l) if n > 0 else tile(-1, b, c, 3, l)
            return full, jnp.where(low, after, before)

        for nh in range(2):
            for ll in range(10):
                c = -1 if ll == 0 else (1 if ll == 9 else 0)
                parts = [[] for _ in range(6)]
                for nl in range(2):
                    n = 2 * nh + nl
                    own = pair(0, c, n, ll - 1)
                    left = pair(-1, c, n, ll - 1)
                    right = pair(1, c, n, ll - 1)
                    for h in range(2):
                        parts[h].append(pltpu.roll(jnp.where(row == 7, left[h], own[h]), 1, 0))
                        parts[2 + h].append(own[h])
                        parts[4 + h].append(pltpu.roll(jnp.where(row == 0, right[h], own[h]), 7, 0))
                for q in range(6):
                    x_ref[s, nh, ll, :, q * 128 : (q + 1) * 128] = jnp.concatenate(
                        parts[q], axis=0
                    ).astype(bf16)
        return carry

    lax.fori_loop(0, CAP, one_slot, 0)


def convolve(x_ref, w_ref, epilogue):
    def one_slot(s, carry):
        total = None
        for c in range(3):
            rows = x_ref[s, :, c : c + E].reshape(256, 768)
            term = jnp.dot(rows, w_ref[c], preferred_element_type=f32)
            total = term if total is None else total + term
        epilogue(pl.ds(pl.multiple_of(s * 256, 256), 256), total)
        return carry

    lax.fori_loop(0, CAP, one_slot, 0)


def logistic(v):
    return 1.0 / (1.0 + jnp.exp(-v))


def conv1_kernel(idx_ref, a_ref, lo_ref, hi_ref, w_ref, x_ref, h_ref, slope_ref, up_ref, down_ref, g_ref, pool_ref):
    build(a_ref, lo_ref, hi_ref, idx_ref, g_ref, pool_ref, x_ref)

    def epilogue(rows, v):
        q = logistic(v)
        h_ref[rows, :] = a_ref[rows, :] + v * q
        slope_ref[rows, :] = q * (1.0 + v * (1.0 - q))

    convolve(x_ref, w_ref, epilogue)
    planes_out(h_ref, up_ref, down_ref)


def conv2_kernel(
    idx_ref, a_ref, lo_ref, hi_ref, w_ref, u_ref, x_ref, o_ref, e_ref, up_ref, down_ref, g_ref, pool_ref
):
    build(a_ref, lo_ref, hi_ref, idx_ref, g_ref, pool_ref, x_ref)

    def epilogue(rows, v):
        q = logistic(v)
        o_ref[rows, :] = a_ref[rows, :] + v * q
        e_ref[rows, :] = u_ref[rows, :] * (q * (1.0 + v * (1.0 - q)))

    convolve(x_ref, w_ref, epilogue)
    planes_out(e_ref, up_ref, down_ref)


def conv3_kernel(
    idx_ref, a_ref, lo_ref, hi_ref, w_ref, u_ref, slope_ref, hg_ref, e_ref, up_ref, down_ref, g_ref, pool_ref, x_ref
):
    build(a_ref, lo_ref, hi_ref, idx_ref, g_ref, pool_ref, x_ref)

    def epilogue(rows, v):
        grad = u_ref[rows, :] + v
        hg_ref[rows, :] = grad
        e_ref[rows, :] = grad * slope_ref[rows, :]

    convolve(x_ref, w_ref, epilogue)
    planes_out(e_ref, up_ref, down_ref)


def conv4_kernel(idx_ref, a_ref, lo_ref, hi_ref, w_ref, hg_ref, o_ref, g_ref, pool_ref, x_ref, r_ref, tmp_ref):
    build(a_ref, lo_ref, hi_ref, idx_ref, g_ref, pool_ref, x_ref)

    def epilogue(rows, v):
        r_ref[rows, :] = hg_ref[rows, :] + v

    convolve(x_ref, w_ref, epilogue)
    from_rows(r_ref, o_ref, tmp_ref)


def weight_grad(x_ref, e_ref, p_ref):
    low = lane_low((C, 128))
    errors = e_ref[...].T.astype(bf16)
    held = None
    for c in range(3):
        rows = x_ref[:, :, c : c + E].reshape(ROWS, 768)
        m = jnp.dot(errors, rows, preferred_element_type=f32)
        for b in range(3):
            number = 3 * c + b
            z0, z1 = m[:C, b * 256 : b * 256 + 128], m[C:, b * 256 : b * 256 + 128]
            y0, y1 = m[:C, b * 256 + 128 : (b + 1) * 256], m[C:, b * 256 + 128 : (b + 1) * 256]
            p_ref[pl.ds(number * C, C), :] = (z0 + pltpu.roll(jnp.where(low, y1, z1), C, 1)).astype(p_ref.dtype)
            if number % 2 == 0:
                held = z1 + pltpu.roll(y0, C, 1)
                if number == 8:
                    p_ref[pl.ds((9 + number // 2) * C, C), :] = jnp.where(low, held, 0.0).astype(p_ref.dtype)
            else:
                odd = pltpu.roll(z1, C, 1) + y0
                p_ref[pl.ds((9 + number // 2) * C, C), :] = jnp.where(low, held, odd).astype(p_ref.dtype)


def w2_kernel(x_ref, e_ref, r_ref, o_ref, p_ref, tmp_ref):
    from_rows(r_ref, o_ref, tmp_ref)
    weight_grad(x_ref, e_ref, p_ref)


def w1_kernel(x_ref, e_ref, p_ref):
    weight_grad(x_ref, e_ref, p_ref)


def finish_kernel(scale, r_ref, first_ref, second_ref):
    for which, ref in enumerate((first_ref, second_ref)):
        for c in range(3):
            for b in range(3):
                number = 3 * c + b
                k = 3 * b + c
                t = (r_ref[pl.ds(which * PACKED + number * C, C), :].astype(f32) * scale).T
                ref[9 + k] = t[:C]
                ref[18 + k] = t[C:]
                if number % 2 == 0:
                    t = (r_ref[pl.ds(which * PACKED + (9 + number // 2) * C, C), :].astype(f32) * scale).T
                    held = t[C:]
                    ref[k] = t[:C]
                else:
                    ref[k] = held


VMEM = pl.BlockSpec(memory_space=pltpu.VMEM)
SMEM = pl.BlockSpec(memory_space=pltpu.SMEM)
FIELD = jax.ShapeDtypeStruct((ROWS, 128), f32)
PLANES = jax.ShapeDtypeStruct((PLANE, 128), bf16)
WINDOWS = (CAP, 2, 10, 16, 768)
WEIGHTS = jax.ShapeDtypeStruct((3, 768, 128), bf16)
CUBES = jax.ShapeDtypeStruct((1, CAP, C, E * E * E), f32)
POOLS = [pltpu.VMEM((ROWS + 256, 128), f32), pltpu.VMEM((2, 2 * PLANE + 32, 128), f32)]
TMP = pltpu.VMEM((16, C, 128), f32)


def call(kernel, name, scalars, arrays, outs, scratch=(), flops=0):
    moved = sum(x.size * x.dtype.itemsize for x in arrays) + sum(o.size * o.dtype.itemsize for o in outs)
    return pl.pallas_call(
        kernel,
        name=name,
        out_shape=outs,
        in_specs=[SMEM] * len(scalars) + [VMEM] * len(arrays),
        out_specs=[VMEM] * len(outs),
        scratch_shapes=list(scratch),
        cost_estimate=pl.CostEstimate(flops=flops, bytes_accessed=moved, transcendentals=0),
        compiler_params=pltpu.CompilerParams(vmem_limit_bytes=24 << 20),
    )(*scalars, *arrays)


def slot_table(neighbours):
    own = neighbours - lax.axis_index("brick") * CAP
    depth = jnp.array([item[2] for item in directions], jnp.int32)[None, :]
    inside = jnp.clip(own, 0, CAP - 1)
    below = jnp.where(own >= 0, inside, jnp.clip(own + 2 * CAP, CAP, 2 * CAP - 1))
    above = jnp.clip(own, 0, 2 * CAP - 1)
    present = neighbours >= 0
    middle = jnp.where(present, inside * 256, ROWS)
    outer = jnp.where(present, jnp.where(depth < 0, below, above) * 32, 2 * PLANE)
    return jnp.where(depth == 0, middle, outer).astype(jnp.int32)


def body(features, cotangent, first_kernel, second_kernel, counts, neighbours):
    bricks = lax.axis_size("brick")
    up_pairs = [(i, (i + 1) % bricks) for i in range(bricks)]
    down_pairs = [(j, i) for i, j in up_pairs]

    def exchange(up, down):
        return lax.ppermute(up, "brick", up_pairs), lax.ppermute(down, "brick", down_pairs)

    idx = slot_table(neighbours)
    windows = jax.ShapeDtypeStruct(WINDOWS, bf16)
    packed = jax.ShapeDtypeStruct((PACKED, 128), bf16)
    scratch_x = pltpu.VMEM(WINDOWS, bf16)
    work = 2 * ROWS * 2304 * 128

    inputs, up, down = call(pre_kernel, "pre", [counts], [features], [FIELD, PLANES, PLANES], [TMP])
    lo, hi = exchange(up, down)
    f1, f2, b1, b2, upstream = call(
        prep_kernel, "prep", [counts], [first_kernel, second_kernel, cotangent], [WEIGHTS] * 4 + [FIELD], [TMP]
    )
    x_in, hidden, slope1, up, down = call(
        conv1_kernel, "conv1", [idx], [inputs, lo, hi, f1], [windows, FIELD, FIELD, PLANES, PLANES], POOLS, work
    )
    lo, hi = exchange(up, down)
    x_hidden, out_rows, second_err, up, down = call(
        conv2_kernel,
        "conv2",
        [idx],
        [hidden, lo, hi, f2, upstream],
        [windows, FIELD, FIELD, PLANES, PLANES],
        POOLS,
        work,
    )
    lo, hi = exchange(up, down)
    outputs, second_local = call(w2_kernel, "w2", [], [x_hidden, second_err, out_rows], [CUBES, packed], [TMP], work)
    hidden_grad, first_err, up, down = call(
        conv3_kernel,
        "conv3",
        [idx],
        [second_err, lo, hi, b2, upstream, slope1],
        [FIELD, FIELD, PLANES, PLANES],
        POOLS + [scratch_x],
        work,
    )
    lo, hi = exchange(up, down)
    (first_local,) = call(w1_kernel, "w1", [], [x_in, first_err], [packed], (), work)
    (input_grad,) = call(
        conv4_kernel,
        "conv4",
        [idx],
        [first_err, lo, hi, b1, hidden_grad],
        [CUBES],
        POOLS + [scratch_x, pltpu.VMEM((ROWS, 128), f32), TMP],
        work,
    )
    axes = ("brick", "scene")
    devices = lax.axis_size("brick") * lax.axis_size("scene")
    share = 2 * PACKED // devices
    partial = jnp.concatenate([first_local, second_local]).reshape(devices, share, 128)
    partial = lax.all_to_all(partial, axes, 0, 0)
    mine = jnp.sum(partial.astype(f32), axis=0).astype(bf16)
    total = lax.all_to_all(jnp.broadcast_to(mine[None], (devices, share, 128)), axes, 0, 0)
    scale = float((devices * CAP * E * E * E) ** -0.5)
    grads = jax.ShapeDtypeStruct((27, C, C), f32)
    first_grad, second_grad = call(
        lambda *refs: finish_kernel(scale, *refs), "finish", [], [total.reshape(2 * PACKED, 128)], [grads, grads]
    )
    return (outputs, input_grad, first_grad, second_grad)


def solution(mesh):
    return jax.shard_map(
        body,
        mesh=mesh,
        in_specs=(
            P("scene", "brick", None, None),
            P("scene", "brick", None, None),
            P(),
            P(),
            P("brick"),
            P("brick", None),
        ),
        out_specs=(P("scene", "brick", None, None), P("scene", "brick", None, None), P(), P()),
        check_vma=False,
    )
```

```python
import jax
import jax.numpy as jnp
from jax import lax
from jax.experimental import pallas as pl
from jax.experimental.pallas import tpu as pltpu
from jax.sharding import PartitionSpec as P

E = 8
C = 64
CAP = 4
f32 = jnp.float32
bf16 = jnp.bfloat16
offsets = [(a, b, c) for a in (-1, 0, 1) for b in (-1, 0, 1) for c in (-1, 0, 1)]
directions = [item for item in offsets if item != (0, 0, 0)]
number_of = {item: n for n, item in enumerate(directions)}

ROWS = CAP * 256
PLANE = CAP * 32
PACKED = 896


def row0(s, n, l):
    return s * 256 + (n // 2) * 128 + l * 16 + (n % 2) * 8


def flip(t):
    tt = t.T
    return jnp.concatenate([tt[:C], tt[C:]], axis=1)


def lane_low(shape):
    return lax.broadcasted_iota(jnp.int32, shape, 1) < C


def to_rows(x_ref, a_ref, tmp_ref, counts_ref):
    for s in range(CAP):
        occupied = jnp.where(s < counts_ref[0], 1.0, 0.0).astype(f32)
        for n in range(4):
            t = x_ref[0, s, :, n * 128 : (n + 1) * 128] * occupied
            tmp_ref[s * 4 + n] = flip(t)
            for l in range(E):
                a_ref[pl.ds(row0(s, n, l), 8), :] = tmp_ref[s * 4 + n, pl.ds(l, 8, stride=8), :]


def from_rows(a_ref, o_ref, tmp_ref):
    for s in range(CAP):
        for n in range(4):
            for l in range(E):
                tmp_ref[s * 4 + n, pl.ds(l, 8, stride=8), :] = a_ref[pl.ds(row0(s, n, l), 8), :]
            o_ref[0, s, :, n * 128 : (n + 1) * 128] = flip(tmp_ref[s * 4 + n])


def planes_out(a_ref, up_ref, down_ref):
    for s in range(CAP):
        for nh in range(2):
            base = s * 256 + nh * 128
            to = pl.ds(s * 32 + nh * 16, 16)
            up_ref[to, :] = a_ref[pl.ds(base + 7 * 16, 16), :].astype(bf16)
            down_ref[to, :] = a_ref[pl.ds(base, 16), :].astype(bf16)


def pre_kernel(counts_ref, x_ref, a_ref, up_ref, down_ref, tmp_ref):
    to_rows(x_ref, a_ref, tmp_ref, counts_ref)
    planes_out(a_ref, up_ref, down_ref)


def flat_weights(w_ref, o_ref, back):
    zero = jnp.zeros((C, C), f32)

    def block(a, b, c):
        k = 9 * (a + 1) + 3 * (b + 1) + (c + 1)
        return w_ref[26 - k].T if back else w_ref[k]

    for ci, c in enumerate((-1, 0, 1)):
        for bi, b in enumerate((-1, 0, 1)):
            low, mid, high = (block(a, b, c) for a in (-1, 0, 1))
            rows = ((mid, low), (high, mid), (zero, high), (low, zero))
            for r, (left, right) in enumerate(rows):
                joined = jnp.concatenate([left, right], axis=1).astype(bf16)
                o_ref[ci, pl.ds(bi * 256 + r * C, C), :] = joined


def prep_kernel(
    counts_ref, w1_hbm, w2_hbm, x_hbm, f1_ref, f2_ref, b1_ref, b2_ref, u_ref, tmp_ref, w1_ref, w2_ref, x_ref, sems
):
    pairs = ((w1_hbm, w1_ref), (w2_hbm, w2_ref), (x_hbm, x_ref))
    copies = [pltpu.make_async_copy(src, dst, sems.at[n]) for n, (src, dst) in enumerate(pairs)]
    for copy in copies:
        copy.start()
    copies[0].wait()
    flat_weights(w1_ref, f1_ref, False)
    flat_weights(w1_ref, b1_ref, True)
    copies[1].wait()
    flat_weights(w2_ref, f2_ref, False)
    flat_weights(w2_ref, b2_ref, True)
    copies[2].wait()
    to_rows(x_ref, u_ref, tmp_ref, counts_ref)


def build(a_ref, lo_ref, hi_ref, idx_ref, g_ref, pool_ref, x_ref):
    g_ref[pl.ds(0, ROWS), :] = a_ref[...]
    g_ref[pl.ds(ROWS, 256), :] = jnp.zeros((256, 128), f32)
    for side, (ref, layer) in enumerate(((lo_ref, 7), (hi_ref, 0))):
        for s in range(CAP):
            for nh in range(2):
                pool_ref[side, pl.ds(s * 32 + nh * 16, 16), :] = a_ref[
                    pl.ds(s * 256 + nh * 128 + layer * 16, 16), :
                ]
        pool_ref[side, pl.ds(PLANE, PLANE), :] = ref[...].astype(f32)
        pool_ref[side, pl.ds(2 * PLANE, 32), :] = jnp.zeros((32, 128), f32)
    row = lax.broadcasted_iota(jnp.int32, (8, 128), 0)
    low = lane_low((8, 128))

    def one_slot(s, carry):
        def tile(a, b, c, n, l):
            nh, nl = n // 2, n % 2
            if (a, b, c) == (0, 0, 0):
                base = s * 256
            else:
                base = idx_ref[s, number_of[a, b, c]]
            if c == 0:
                return g_ref[pl.ds(pl.multiple_of(base + (nh * 128 + l * 16 + nl * 8), 8), 8), :]
            side = 0 if c < 0 else 1
            return pool_ref[side, pl.ds(pl.multiple_of(base + (nh * 16 + nl * 8), 8), 8), :]

        def pair(b, c, n, l):
            full = tile(0, b, c, n, l)
            after = tile(0, b, c, n + 1, l) if n < 3 else tile(1, b, c, 0, l)
            before = tile(0, b, c, n - 1, l) if n > 0 else tile(-1, b, c, 3, l)
            return full, jnp.where(low, after, before)

        for nh in range(2):
            for ll in range(10):
                c = -1 if ll == 0 else (1 if ll == 9 else 0)
                parts = [[] for _ in range(6)]
                for nl in range(2):
                    n = 2 * nh + nl
                    own = pair(0, c, n, ll - 1)
                    left = pair(-1, c, n, ll - 1)
                    right = pair(1, c, n, ll - 1)
                    for h in range(2):
                        parts[h].append(pltpu.roll(jnp.where(row == 7, left[h], own[h]), 1, 0))
                        parts[2 + h].append(own[h])
                        parts[4 + h].append(pltpu.roll(jnp.where(row == 0, right[h], own[h]), 7, 0))
                for q in range(6):
                    x_ref[s, nh, ll, :, q * 128 : (q + 1) * 128] = jnp.concatenate(
                        parts[q], axis=0
                    ).astype(bf16)
        return carry

    lax.fori_loop(0, CAP, one_slot, 0)


def convolve(x_ref, w_ref, epilogue):
    def one_slot(s, carry):
        total = None
        for c in range(3):
            rows = x_ref[s, :, c : c + E].reshape(256, 768)
            term = jnp.dot(rows, w_ref[c], preferred_element_type=f32)
            total = term if total is None else total + term
        epilogue(pl.ds(pl.multiple_of(s * 256, 256), 256), total)
        return carry

    lax.fori_loop(0, CAP, one_slot, 0)


def logistic(v):
    return 1.0 / (1.0 + jnp.exp(-v))


def conv1_kernel(idx_ref, a_ref, lo_ref, hi_ref, w_ref, x_ref, h_ref, slope_ref, up_ref, down_ref, g_ref, pool_ref):
    build(a_ref, lo_ref, hi_ref, idx_ref, g_ref, pool_ref, x_ref)

    def epilogue(rows, v):
        q = logistic(v)
        h_ref[rows, :] = a_ref[rows, :] + v * q
        slope_ref[rows, :] = q * (1.0 + v * (1.0 - q))

    convolve(x_ref, w_ref, epilogue)
    planes_out(h_ref, up_ref, down_ref)


def conv2_kernel(
    idx_ref, a_ref, lo_ref, hi_ref, w_ref, u_ref, x_ref, o_ref, e_ref, up_ref, down_ref, g_ref, pool_ref
):
    build(a_ref, lo_ref, hi_ref, idx_ref, g_ref, pool_ref, x_ref)

    def epilogue(rows, v):
        q = logistic(v)
        o_ref[rows, :] = a_ref[rows, :] + v * q
        e_ref[rows, :] = u_ref[rows, :] * (q * (1.0 + v * (1.0 - q)))

    convolve(x_ref, w_ref, epilogue)
    planes_out(e_ref, up_ref, down_ref)


def conv3_kernel(
    idx_ref, a_ref, lo_ref, hi_ref, w_ref, u_ref, slope_ref, hg_ref, e_ref, up_ref, down_ref, g_ref, pool_ref, x_ref
):
    build(a_ref, lo_ref, hi_ref, idx_ref, g_ref, pool_ref, x_ref)

    def epilogue(rows, v):
        grad = u_ref[rows, :] + v
        hg_ref[rows, :] = grad
        e_ref[rows, :] = grad * slope_ref[rows, :]

    convolve(x_ref, w_ref, epilogue)
    planes_out(e_ref, up_ref, down_ref)


def conv4_kernel(idx_ref, a_ref, lo_ref, hi_ref, w_ref, hg_ref, o_ref, g_ref, pool_ref, x_ref, r_ref, tmp_ref):
    build(a_ref, lo_ref, hi_ref, idx_ref, g_ref, pool_ref, x_ref)

    def epilogue(rows, v):
        r_ref[rows, :] = hg_ref[rows, :] + v

    convolve(x_ref, w_ref, epilogue)
    from_rows(r_ref, o_ref, tmp_ref)


def weight_grad(x_ref, e_ref, p_ref):
    low = lane_low((C, 128))
    errors = e_ref[...].T.astype(bf16)
    held = None
    for c in range(3):
        rows = x_ref[:, :, c : c + E].reshape(ROWS, 768)
        m = jnp.dot(errors, rows, preferred_element_type=f32)
        for b in range(3):
            number = 3 * c + b
            z0, z1 = m[:C, b * 256 : b * 256 + 128], m[C:, b * 256 : b * 256 + 128]
            y0, y1 = m[:C, b * 256 + 128 : (b + 1) * 256], m[C:, b * 256 + 128 : (b + 1) * 256]
            p_ref[pl.ds(number * C, C), :] = (z0 + pltpu.roll(jnp.where(low, y1, z1), C, 1)).astype(p_ref.dtype)
            if number % 2 == 0:
                held = z1 + pltpu.roll(y0, C, 1)
                if number == 8:
                    p_ref[pl.ds((9 + number // 2) * C, C), :] = jnp.where(low, held, 0.0).astype(p_ref.dtype)
            else:
                odd = pltpu.roll(z1, C, 1) + y0
                p_ref[pl.ds((9 + number // 2) * C, C), :] = jnp.where(low, held, odd).astype(p_ref.dtype)


def w2_kernel(x_ref, e_ref, r_ref, o_ref, p_ref, tmp_ref):
    from_rows(r_ref, o_ref, tmp_ref)
    weight_grad(x_ref, e_ref, p_ref)


def w1_kernel(x_ref, e_ref, p_ref):
    weight_grad(x_ref, e_ref, p_ref)


def finish_kernel(scale, r_ref, first_ref, second_ref):
    for which, ref in enumerate((first_ref, second_ref)):
        for c in range(3):
            for b in range(3):
                number = 3 * c + b
                k = 3 * b + c
                t = (r_ref[pl.ds(which * PACKED + number * C, C), :].astype(f32) * scale).T
                ref[9 + k] = t[:C]
                ref[18 + k] = t[C:]
                if number % 2 == 0:
                    t = (r_ref[pl.ds(which * PACKED + (9 + number // 2) * C, C), :].astype(f32) * scale).T
                    held = t[C:]
                    ref[k] = t[:C]
                else:
                    ref[k] = held


VMEM = pl.BlockSpec(memory_space=pltpu.VMEM)
SMEM = pl.BlockSpec(memory_space=pltpu.SMEM)
HBM = pl.BlockSpec(memory_space=pltpu.HBM)
FIELD = jax.ShapeDtypeStruct((ROWS, 128), f32)
PLANES = jax.ShapeDtypeStruct((PLANE, 128), bf16)
WINDOWS = (CAP, 2, 10, 16, 768)
WEIGHTS = jax.ShapeDtypeStruct((3, 768, 128), bf16)
CUBES = jax.ShapeDtypeStruct((1, CAP, C, E * E * E), f32)
POOLS = [pltpu.VMEM((ROWS + 256, 128), f32), pltpu.VMEM((2, 2 * PLANE + 32, 128), f32)]
TMP = pltpu.VMEM((16, C, 128), f32)


def call(kernel, name, scalars, arrays, outs, scratch=(), flops=0, place=VMEM):
    moved = sum(x.size * x.dtype.itemsize for x in arrays) + sum(o.size * o.dtype.itemsize for o in outs)
    return pl.pallas_call(
        kernel,
        name=name,
        out_shape=outs,
        in_specs=[SMEM] * len(scalars) + [place] * len(arrays),
        out_specs=[VMEM] * len(outs),
        scratch_shapes=list(scratch),
        cost_estimate=pl.CostEstimate(flops=flops, bytes_accessed=moved, transcendentals=0),
        compiler_params=pltpu.CompilerParams(vmem_limit_bytes=24 << 20),
    )(*scalars, *arrays)


def slot_table(neighbours):
    own = neighbours - lax.axis_index("brick") * CAP
    depth = jnp.array([item[2] for item in directions], jnp.int32)[None, :]
    inside = jnp.clip(own, 0, CAP - 1)
    below = jnp.where(own >= 0, inside, jnp.clip(own + 2 * CAP, CAP, 2 * CAP - 1))
    above = jnp.clip(own, 0, 2 * CAP - 1)
    present = neighbours >= 0
    middle = jnp.where(present, inside * 256, ROWS)
    outer = jnp.where(present, jnp.where(depth < 0, below, above) * 32, 2 * PLANE)
    return jnp.where(depth == 0, middle, outer).astype(jnp.int32)


def body(features, cotangent, first_kernel, second_kernel, counts, neighbours):
    bricks = lax.axis_size("brick")
    up_pairs = [(i, (i + 1) % bricks) for i in range(bricks)]
    down_pairs = [(j, i) for i, j in up_pairs]

    def exchange(up, down):
        return lax.ppermute(up, "brick", up_pairs), lax.ppermute(down, "brick", down_pairs)

    idx = slot_table(neighbours)
    windows = jax.ShapeDtypeStruct(WINDOWS, bf16)
    packed = jax.ShapeDtypeStruct((PACKED, 128), bf16)
    scratch_x = pltpu.VMEM(WINDOWS, bf16)
    work = 2 * ROWS * 2304 * 128

    inputs, up, down = call(pre_kernel, "pre", [counts], [features], [FIELD, PLANES, PLANES], [TMP])
    lo, hi = exchange(up, down)
    f1, f2, b1, b2, upstream = call(
        prep_kernel,
        "prep",
        [counts],
        [pltpu.with_memory_space_constraint(v, pltpu.HBM) for v in (first_kernel, second_kernel, cotangent)],
        [WEIGHTS] * 4 + [FIELD],
        [
            TMP,
            pltpu.VMEM((27, C, C), f32),
            pltpu.VMEM((27, C, C), f32),
            pltpu.VMEM((1, CAP, C, E * E * E), f32),
            pltpu.SemaphoreType.DMA((3,)),
        ],
        place=HBM,
    )
    x_in, hidden, slope1, up, down = call(
        conv1_kernel, "conv1", [idx], [inputs, lo, hi, f1], [windows, FIELD, FIELD, PLANES, PLANES], POOLS, work
    )
    lo, hi = exchange(up, down)
    x_hidden, out_rows, second_err, up, down = call(
        conv2_kernel,
        "conv2",
        [idx],
        [hidden, lo, hi, f2, upstream],
        [windows, FIELD, FIELD, PLANES, PLANES],
        POOLS,
        work,
    )
    lo, hi = exchange(up, down)
    outputs, second_local = call(w2_kernel, "w2", [], [x_hidden, second_err, out_rows], [CUBES, packed], [TMP], work)
    hidden_grad, first_err, up, down = call(
        conv3_kernel,
        "conv3",
        [idx],
        [second_err, lo, hi, b2, upstream, slope1],
        [FIELD, FIELD, PLANES, PLANES],
        POOLS + [scratch_x],
        work,
    )
    lo, hi = exchange(up, down)
    (first_local,) = call(w1_kernel, "w1", [], [x_in, first_err], [packed], (), work)
    (input_grad,) = call(
        conv4_kernel,
        "conv4",
        [idx],
        [first_err, lo, hi, b1, hidden_grad],
        [CUBES],
        POOLS + [scratch_x, pltpu.VMEM((ROWS, 128), f32), TMP],
        work,
    )
    axes = ("brick", "scene")
    scenes = lax.axis_size("scene")
    devices = bricks * scenes
    row = 4 if bricks % 4 == 0 else 1
    near, far = row * scenes, bricks // row
    near_groups = [list(range(z * near, (z + 1) * near)) for z in range(far)]
    far_groups = [[x + row * z for z in range(far)] for x in range(row)]
    share = 2 * PACKED // near

    def near_exchange(blocks):
        return lax.all_to_all(blocks, axes, 0, 0, axis_index_groups=near_groups, tiled=True)

    def far_exchange(blocks):
        return lax.all_to_all(blocks, "brick", 0, 0, axis_index_groups=far_groups, tiled=True)

    def total_of(blocks):
        return jnp.sum(blocks.astype(f32), axis=0).astype(bf16)

    def spread(block, count):
        return jnp.broadcast_to(block[None], (count,) + block.shape)

    partial = jnp.concatenate([first_local, second_local]).reshape(near, share, 128)
    mine = total_of(near_exchange(partial))
    mine = total_of(far_exchange(spread(mine, far)))
    total = near_exchange(spread(mine, near))
    scale = float((devices * CAP * E * E * E) ** -0.5)
    grads = jax.ShapeDtypeStruct((27, C, C), f32)
    first_grad, second_grad = call(
        lambda *refs: finish_kernel(scale, *refs), "finish", [], [total.reshape(2 * PACKED, 128)], [grads, grads]
    )
    return (outputs, input_grad, first_grad, second_grad)


def solution(mesh):
    return jax.shard_map(
        body,
        mesh=mesh,
        in_specs=(
            P("scene", "brick", None, None),
            P("scene", "brick", None, None),
            P(),
            P(),
            P("brick"),
            P("brick", None),
        ),
        out_specs=(P("scene", "brick", None, None), P("scene", "brick", None, None), P(), P()),
        check_vma=False,
    )
```

```python
import jax
import jax.numpy as jnp
from jax import lax
from jax.experimental import pallas as pl
from jax.experimental.pallas import tpu as pltpu
from jax.sharding import PartitionSpec as P

E = 8
C = 64
CAP = 4
f32 = jnp.float32
bf16 = jnp.bfloat16
offsets = [(a, b, c) for a in (-1, 0, 1) for b in (-1, 0, 1) for c in (-1, 0, 1)]
directions = [item for item in offsets if item != (0, 0, 0)]
number_of = {item: n for n, item in enumerate(directions)}

ROWS = CAP * 256
PLANE = CAP * 32
PACKED = 896


def row0(s, n, l):
    return s * 256 + (n // 2) * 128 + l * 16 + (n % 2) * 8


def flip(t):
    tt = t.T
    return jnp.concatenate([tt[:C], tt[C:]], axis=1)


def lane_low(shape):
    return lax.broadcasted_iota(jnp.int32, shape, 1) < C


def to_rows(x_ref, a_ref, tmp_ref, counts_ref):
    for s in range(CAP):
        occupied = jnp.where(s < counts_ref[0], 1.0, 0.0).astype(f32)
        for n in range(4):
            t = x_ref[0, s, :, n * 128 : (n + 1) * 128] * occupied
            tmp_ref[s * 4 + n] = flip(t)
            for l in range(E):
                a_ref[pl.ds(row0(s, n, l), 8), :] = tmp_ref[s * 4 + n, pl.ds(l, 8, stride=8), :]


def from_rows(a_ref, o_ref, tmp_ref):
    for s in range(CAP):
        for n in range(4):
            for l in range(E):
                tmp_ref[s * 4 + n, pl.ds(l, 8, stride=8), :] = a_ref[pl.ds(row0(s, n, l), 8), :]
            o_ref[0, s, :, n * 128 : (n + 1) * 128] = flip(tmp_ref[s * 4 + n])


def planes_out(a_ref, up_ref, down_ref):
    for s in range(CAP):
        for nh in range(2):
            base = s * 256 + nh * 128
            to = pl.ds(s * 32 + nh * 16, 16)
            up_ref[to, :] = a_ref[pl.ds(base + 7 * 16, 16), :].astype(bf16)
            down_ref[to, :] = a_ref[pl.ds(base, 16), :].astype(bf16)


def pre_kernel(counts_ref, x_ref, a_ref, up_ref, down_ref, tmp_ref):
    to_rows(x_ref, a_ref, tmp_ref, counts_ref)
    planes_out(a_ref, up_ref, down_ref)


def flat_weights(w_ref, o_ref, back):
    zero = jnp.zeros((C, C), f32)

    def block(a, b, c):
        k = 9 * (a + 1) + 3 * (b + 1) + (c + 1)
        return w_ref[26 - k].T if back else w_ref[k]

    for ci, c in enumerate((-1, 0, 1)):
        for bi, b in enumerate((-1, 0, 1)):
            low, mid, high = (block(a, b, c) for a in (-1, 0, 1))
            rows = ((mid, low), (high, mid), (zero, high), (low, zero))
            for r, (left, right) in enumerate(rows):
                joined = jnp.concatenate([left, right], axis=1).astype(bf16)
                o_ref[ci, pl.ds(bi * 256 + r * C, C), :] = joined


def prep_kernel(
    counts_ref, w1_hbm, w2_hbm, x_hbm, f1_ref, f2_ref, b1_ref, b2_ref, u_ref, tmp_ref, w1_ref, w2_ref, x_ref, sems
):
    pairs = ((w1_hbm, w1_ref), (w2_hbm, w2_ref), (x_hbm, x_ref))
    copies = [pltpu.make_async_copy(src, dst, sems.at[n]) for n, (src, dst) in enumerate(pairs)]
    for copy in copies:
        copy.start()
    copies[0].wait()
    flat_weights(w1_ref, f1_ref, False)
    flat_weights(w1_ref, b1_ref, True)
    copies[1].wait()
    flat_weights(w2_ref, f2_ref, False)
    flat_weights(w2_ref, b2_ref, True)
    copies[2].wait()
    to_rows(x_ref, u_ref, tmp_ref, counts_ref)


def build(a_ref, lo_ref, hi_ref, idx_ref, g_ref, pool_ref, x_ref):
    g_ref[pl.ds(0, ROWS), :] = a_ref[...]
    g_ref[pl.ds(ROWS, 256), :] = jnp.zeros((256, 128), f32)
    for side, (ref, layer) in enumerate(((lo_ref, 7), (hi_ref, 0))):
        for s in range(CAP):
            for nh in range(2):
                pool_ref[side, pl.ds(s * 32 + nh * 16, 16), :] = a_ref[
                    pl.ds(s * 256 + nh * 128 + layer * 16, 16), :
                ]
        pool_ref[side, pl.ds(PLANE, PLANE), :] = ref[...].astype(f32)
        pool_ref[side, pl.ds(2 * PLANE, 32), :] = jnp.zeros((32, 128), f32)
    row = lax.broadcasted_iota(jnp.int32, (8, 128), 0)
    low = lane_low((8, 128))

    def one_slot(s, carry):
        def tile(a, b, c, n, l):
            nh, nl = n // 2, n % 2
            if (a, b, c) == (0, 0, 0):
                base = s * 256
            else:
                base = idx_ref[s, number_of[a, b, c]]
            if c == 0:
                return g_ref[pl.ds(pl.multiple_of(base + (nh * 128 + l * 16 + nl * 8), 8), 8), :]
            side = 0 if c < 0 else 1
            return pool_ref[side, pl.ds(pl.multiple_of(base + (nh * 16 + nl * 8), 8), 8), :]

        def pair(b, c, n, l):
            full = tile(0, b, c, n, l)
            after = tile(0, b, c, n + 1, l) if n < 3 else tile(1, b, c, 0, l)
            before = tile(0, b, c, n - 1, l) if n > 0 else tile(-1, b, c, 3, l)
            return full, jnp.where(low, after, before)

        for nh in range(2):
            for ll in range(10):
                c = -1 if ll == 0 else (1 if ll == 9 else 0)
                parts = [[] for _ in range(6)]
                for nl in range(2):
                    n = 2 * nh + nl
                    own = pair(0, c, n, ll - 1)
                    left = pair(-1, c, n, ll - 1)
                    right = pair(1, c, n, ll - 1)
                    for h in range(2):
                        parts[h].append(pltpu.roll(jnp.where(row == 7, left[h], own[h]), 1, 0))
                        parts[2 + h].append(own[h])
                        parts[4 + h].append(pltpu.roll(jnp.where(row == 0, right[h], own[h]), 7, 0))
                for q in range(6):
                    x_ref[s, nh, ll, :, q * 128 : (q + 1) * 128] = jnp.concatenate(
                        parts[q], axis=0
                    ).astype(bf16)
        return carry

    lax.fori_loop(0, CAP, one_slot, 0)


def convolve(x_ref, w_ref, epilogue):
    def one_slot(s, carry):
        total = None
        for c in range(3):
            rows = x_ref[s, :, c : c + E].reshape(256, 768)
            term = jnp.dot(rows, w_ref[c], preferred_element_type=f32)
            total = term if total is None else total + term
        epilogue(pl.ds(pl.multiple_of(s * 256, 256), 256), total)
        return carry

    lax.fori_loop(0, CAP, one_slot, 0)


def logistic(v):
    return 1.0 / (1.0 + jnp.exp(-v))


def conv1_kernel(idx_ref, a_ref, lo_ref, hi_ref, w_ref, x_ref, h_ref, slope_ref, up_ref, down_ref, g_ref, pool_ref):
    build(a_ref, lo_ref, hi_ref, idx_ref, g_ref, pool_ref, x_ref)

    def epilogue(rows, v):
        q = logistic(v)
        h_ref[rows, :] = a_ref[rows, :] + v * q
        slope_ref[rows, :] = q * (1.0 + v * (1.0 - q))

    convolve(x_ref, w_ref, epilogue)
    planes_out(h_ref, up_ref, down_ref)


def conv2_kernel(
    idx_ref, a_ref, lo_ref, hi_ref, w_ref, u_ref, x_ref, o_ref, e_ref, up_ref, down_ref, g_ref, pool_ref
):
    build(a_ref, lo_ref, hi_ref, idx_ref, g_ref, pool_ref, x_ref)

    def epilogue(rows, v):
        q = logistic(v)
        o_ref[rows, :] = a_ref[rows, :] + v * q
        e_ref[rows, :] = u_ref[rows, :] * (q * (1.0 + v * (1.0 - q)))

    convolve(x_ref, w_ref, epilogue)
    planes_out(e_ref, up_ref, down_ref)


def conv3_kernel(
    idx_ref, a_ref, lo_ref, hi_ref, w_ref, u_ref, slope_ref, hg_ref, e_ref, up_ref, down_ref, g_ref, pool_ref, x_ref
):
    build(a_ref, lo_ref, hi_ref, idx_ref, g_ref, pool_ref, x_ref)

    def epilogue(rows, v):
        grad = u_ref[rows, :] + v
        hg_ref[rows, :] = grad
        e_ref[rows, :] = grad * slope_ref[rows, :]

    convolve(x_ref, w_ref, epilogue)
    planes_out(e_ref, up_ref, down_ref)


def conv4_kernel(idx_ref, a_ref, lo_ref, hi_ref, w_ref, hg_ref, o_ref, g_ref, pool_ref, x_ref, r_ref, tmp_ref):
    build(a_ref, lo_ref, hi_ref, idx_ref, g_ref, pool_ref, x_ref)

    def epilogue(rows, v):
        r_ref[rows, :] = hg_ref[rows, :] + v

    convolve(x_ref, w_ref, epilogue)
    from_rows(r_ref, o_ref, tmp_ref)


def weight_grad(x_ref, e_ref, p_ref):
    low = lane_low((C, 128))
    errors = e_ref[...].T.astype(bf16)
    held = None
    for c in range(3):
        rows = x_ref[:, :, c : c + E].reshape(ROWS, 768)
        m = jnp.dot(errors, rows, preferred_element_type=f32)
        for b in range(3):
            number = 3 * c + b
            z0, z1 = m[:C, b * 256 : b * 256 + 128], m[C:, b * 256 : b * 256 + 128]
            y0, y1 = m[:C, b * 256 + 128 : (b + 1) * 256], m[C:, b * 256 + 128 : (b + 1) * 256]
            p_ref[pl.ds(number * C, C), :] = (z0 + pltpu.roll(jnp.where(low, y1, z1), C, 1)).astype(p_ref.dtype)
            if number % 2 == 0:
                held = z1 + pltpu.roll(y0, C, 1)
                if number == 8:
                    p_ref[pl.ds((9 + number // 2) * C, C), :] = jnp.where(low, held, 0.0).astype(p_ref.dtype)
            else:
                odd = pltpu.roll(z1, C, 1) + y0
                p_ref[pl.ds((9 + number // 2) * C, C), :] = jnp.where(low, held, odd).astype(p_ref.dtype)


def w2_kernel(x_ref, e_ref, r_ref, o_ref, p_ref, tmp_ref):
    from_rows(r_ref, o_ref, tmp_ref)
    weight_grad(x_ref, e_ref, p_ref)


def w1_kernel(x_ref, e_ref, p_ref):
    weight_grad(x_ref, e_ref, p_ref)


def finish_kernel(scale, r_ref, first_ref, second_ref):
    for which, ref in enumerate((first_ref, second_ref)):
        for c in range(3):
            for b in range(3):
                number = 3 * c + b
                k = 3 * b + c
                t = (r_ref[pl.ds(which * PACKED + number * C, C), :].astype(f32) * scale).T
                ref[9 + k] = t[:C]
                ref[18 + k] = t[C:]
                if number % 2 == 0:
                    t = (r_ref[pl.ds(which * PACKED + (9 + number // 2) * C, C), :].astype(f32) * scale).T
                    held = t[C:]
                    ref[k] = t[:C]
                else:
                    ref[k] = held


VMEM = pl.BlockSpec(memory_space=pltpu.VMEM)
SMEM = pl.BlockSpec(memory_space=pltpu.SMEM)
HBM = pl.BlockSpec(memory_space=pltpu.HBM)
FIELD = jax.ShapeDtypeStruct((ROWS, 128), f32)
PLANES = jax.ShapeDtypeStruct((PLANE, 128), bf16)
WINDOWS = (CAP, 2, 10, 16, 768)
WEIGHTS = jax.ShapeDtypeStruct((3, 768, 128), bf16)
CUBES = jax.ShapeDtypeStruct((1, CAP, C, E * E * E), f32)
POOLS = [pltpu.VMEM((ROWS + 256, 128), f32), pltpu.VMEM((2, 2 * PLANE + 32, 128), f32)]
TMP = pltpu.VMEM((16, C, 128), f32)


def call(kernel, name, scalars, arrays, outs, scratch=(), flops=0, place=VMEM):
    moved = sum(x.size * x.dtype.itemsize for x in arrays) + sum(o.size * o.dtype.itemsize for o in outs)
    return pl.pallas_call(
        kernel,
        name=name,
        out_shape=outs,
        in_specs=[SMEM] * len(scalars) + [place] * len(arrays),
        out_specs=[VMEM] * len(outs),
        scratch_shapes=list(scratch),
        cost_estimate=pl.CostEstimate(flops=flops, bytes_accessed=moved, transcendentals=0),
        compiler_params=pltpu.CompilerParams(vmem_limit_bytes=24 << 20),
    )(*scalars, *arrays)


def slot_table(neighbours):
    own = neighbours - lax.axis_index("brick") * CAP
    depth = jnp.array([item[2] for item in directions], jnp.int32)[None, :]
    inside = jnp.clip(own, 0, CAP - 1)
    below = jnp.where(own >= 0, inside, jnp.clip(own + 2 * CAP, CAP, 2 * CAP - 1))
    above = jnp.clip(own, 0, 2 * CAP - 1)
    present = neighbours >= 0
    middle = jnp.where(present, inside * 256, ROWS)
    outer = jnp.where(present, jnp.where(depth < 0, below, above) * 32, 2 * PLANE)
    return jnp.where(depth == 0, middle, outer).astype(jnp.int32)


def body(features, cotangent, first_kernel, second_kernel, counts, neighbours):
    bricks = lax.axis_size("brick")
    up_pairs = [(i, (i + 1) % bricks) for i in range(bricks)]
    down_pairs = [(j, i) for i, j in up_pairs]

    def exchange(up, down):
        return lax.ppermute(up, "brick", up_pairs), lax.ppermute(down, "brick", down_pairs)

    idx = slot_table(neighbours)
    windows = jax.ShapeDtypeStruct(WINDOWS, bf16)
    packed = jax.ShapeDtypeStruct((PACKED, 128), bf16)
    scratch_x = pltpu.VMEM(WINDOWS, bf16)
    work = 2 * ROWS * 2304 * 128

    inputs, up, down = call(pre_kernel, "pre", [counts], [features], [FIELD, PLANES, PLANES], [TMP])
    lo, hi = exchange(up, down)
    f1, f2, b1, b2, upstream = call(
        prep_kernel,
        "prep",
        [counts],
        [pltpu.with_memory_space_constraint(v, pltpu.HBM) for v in (first_kernel, second_kernel, cotangent)],
        [WEIGHTS] * 4 + [FIELD],
        [
            TMP,
            pltpu.VMEM((27, C, C), f32),
            pltpu.VMEM((27, C, C), f32),
            pltpu.VMEM((1, CAP, C, E * E * E), f32),
            pltpu.SemaphoreType.DMA((3,)),
        ],
        place=HBM,
    )
    x_in, hidden, slope1, up, down = call(
        conv1_kernel, "conv1", [idx], [inputs, lo, hi, f1], [windows, FIELD, FIELD, PLANES, PLANES], POOLS, work
    )
    lo, hi = exchange(up, down)
    x_hidden, out_rows, second_err, up, down = call(
        conv2_kernel,
        "conv2",
        [idx],
        [hidden, lo, hi, f2, upstream],
        [windows, FIELD, FIELD, PLANES, PLANES],
        POOLS,
        work,
    )
    lo, hi = exchange(up, down)
    outputs, second_local = call(w2_kernel, "w2", [], [x_hidden, second_err, out_rows], [CUBES, packed], [TMP], work)
    hidden_grad, first_err, up, down = call(
        conv3_kernel,
        "conv3",
        [idx],
        [second_err, lo, hi, b2, upstream, slope1],
        [FIELD, FIELD, PLANES, PLANES],
        POOLS + [scratch_x],
        work,
    )
    lo, hi = exchange(up, down)
    (first_local,) = call(w1_kernel, "w1", [], [x_in, first_err], [packed], (), work)
    (input_grad,) = call(
        conv4_kernel,
        "conv4",
        [idx],
        [first_err, lo, hi, b1, hidden_grad],
        [CUBES],
        POOLS + [scratch_x, pltpu.VMEM((ROWS, 128), f32), TMP],
        work,
    )
    axes = ("brick", "scene")
    scenes = lax.axis_size("scene")
    devices = bricks * scenes
    row = 4 if bricks % 4 == 0 else 1
    near, far = row * scenes, bricks // row
    near_groups = [list(range(z * near, (z + 1) * near)) for z in range(far)]
    far_groups = [[x + row * z for z in range(far)] for x in range(row)]
    share = 2 * PACKED // near

    def near_exchange(blocks):
        return lax.all_to_all(blocks, axes, 0, 0, axis_index_groups=near_groups, tiled=True)

    def far_exchange(blocks):
        return lax.all_to_all(blocks, "brick", 0, 0, axis_index_groups=far_groups, tiled=True)

    def total_of(blocks):
        return jnp.sum(blocks.astype(f32), axis=0).astype(bf16)

    def spread(block, count):
        return jnp.broadcast_to(block[None], (count,) + block.shape)

    partial = jnp.concatenate([first_local, second_local]).reshape(near, share, 128)
    mine, input_grad = lax.optimization_barrier((total_of(near_exchange(partial)), input_grad))
    mine = total_of(far_exchange(spread(mine, far)))
    total = near_exchange(spread(mine, near))
    scale = float((devices * CAP * E * E * E) ** -0.5)
    grads = jax.ShapeDtypeStruct((27, C, C), f32)
    first_grad, second_grad = call(
        lambda *refs: finish_kernel(scale, *refs), "finish", [], [total.reshape(2 * PACKED, 128)], [grads, grads]
    )
    return (outputs, input_grad, first_grad, second_grad)


def solution(mesh):
    return jax.shard_map(
        body,
        mesh=mesh,
        in_specs=(
            P("scene", "brick", None, None),
            P("scene", "brick", None, None),
            P(),
            P(),
            P("brick"),
            P("brick", None),
        ),
        out_specs=(P("scene", "brick", None, None), P("scene", "brick", None, None), P(), P()),
        check_vma=False,
    )
```

```python
import jax
import jax.numpy as jnp
from jax import lax
from jax.experimental import pallas as pl
from jax.experimental.pallas import tpu as pltpu
from jax.sharding import PartitionSpec as P


E = 8
C = 64
CAP = 4
f32 = jnp.float32
bf16 = jnp.bfloat16
offsets = [(a, b, c) for a in (-1, 0, 1) for b in (-1, 0, 1) for c in (-1, 0, 1)]
directions = [item for item in offsets if item != (0, 0, 0)]
number_of = {item: n for n, item in enumerate(directions)}

ROWS = CAP * 256
PLANE = CAP * 32
PACKED = 896


def row0(s, n, l):
    return s * 256 + (n // 2) * 128 + l * 16 + (n % 2) * 8


def flip(t):
    tt = t.T
    return jnp.concatenate([tt[:C], tt[C:]], axis=1)


def lane_low(shape):
    return lax.broadcasted_iota(jnp.int32, shape, 1) < C


def to_rows(x_ref, a_ref, tmp_ref, counts_ref):
    for s in range(CAP):
        occupied = jnp.where(s < counts_ref[0], 1.0, 0.0).astype(f32)
        for n in range(4):
            t = x_ref[0, s, :, n * 128 : (n + 1) * 128] * occupied
            tmp_ref[s * 4 + n] = flip(t)
            for l in range(E):
                a_ref[pl.ds(row0(s, n, l), 8), :] = tmp_ref[s * 4 + n, pl.ds(l, 8, stride=8), :]


def from_rows(a_ref, o_ref, tmp_ref):
    for s in range(CAP):
        for n in range(4):
            for l in range(E):
                tmp_ref[s * 4 + n, pl.ds(l, 8, stride=8), :] = a_ref[pl.ds(row0(s, n, l), 8), :]
            o_ref[0, s, :, n * 128 : (n + 1) * 128] = flip(tmp_ref[s * 4 + n])


def planes_out(a_ref, up_ref, down_ref):
    for s in range(CAP):
        for nh in range(2):
            base = s * 256 + nh * 128
            to = pl.ds(s * 32 + nh * 16, 16)
            up_ref[to, :] = a_ref[pl.ds(base + 7 * 16, 16), :].astype(bf16)
            down_ref[to, :] = a_ref[pl.ds(base, 16), :].astype(bf16)


def pre_kernel(counts_ref, x_ref, a_ref, up_ref, down_ref, tmp_ref):
    to_rows(x_ref, a_ref, tmp_ref, counts_ref)
    planes_out(a_ref, up_ref, down_ref)


def flat_weights(w_ref, o_ref, back):
    zero = jnp.zeros((C, C), f32)

    def block(a, b, c):
        k = 9 * (a + 1) + 3 * (b + 1) + (c + 1)
        return w_ref[26 - k].T if back else w_ref[k]

    blank = jnp.zeros((256, 128), bf16)
    for bi, b in enumerate((-1, 0, 1)):
        rows = pl.ds(bi * 256, 256)
        o_ref[0, rows, 128:] = blank
        o_ref[3, rows, :128] = blank
        for ci, c in enumerate((-1, 0, 1)):
            low, mid, high = (block(a, b, c) for a in (-1, 0, 1))
            left = jnp.concatenate([mid, high, zero, low], axis=0)
            right = jnp.concatenate([low, mid, high, zero], axis=0)
            joined = jnp.concatenate([left, right], axis=1).astype(bf16)
            o_ref[ci, rows, :128] = joined
            o_ref[ci + 1, rows, 128:] = joined


def prep_kernel(
    counts_ref, w1_hbm, w2_hbm, x_hbm, f1_ref, f2_ref, b1_ref, b2_ref, u_ref, tmp_ref, w1_ref, w2_ref, x_ref, sems
):
    pairs = ((w1_hbm, w1_ref), (w2_hbm, w2_ref), (x_hbm, x_ref))
    copies = [pltpu.make_async_copy(src, dst, sems.at[n]) for n, (src, dst) in enumerate(pairs)]
    for copy in copies:
        copy.start()
    copies[0].wait()
    flat_weights(w1_ref, f1_ref, False)
    flat_weights(w1_ref, b1_ref, True)
    copies[1].wait()
    flat_weights(w2_ref, f2_ref, False)
    flat_weights(w2_ref, b2_ref, True)
    copies[2].wait()
    to_rows(x_ref, u_ref, tmp_ref, counts_ref)


def build(a_ref, lo_ref, hi_ref, idx_ref, g_ref, pool_ref, x_ref):
    g_ref[pl.ds(0, ROWS), :] = a_ref[...]
    g_ref[pl.ds(ROWS, 256), :] = jnp.zeros((256, 128), f32)
    for side, (ref, layer) in enumerate(((lo_ref, 7), (hi_ref, 0))):
        for s in range(CAP):
            for nh in range(2):
                pool_ref[side, pl.ds(s * 32 + nh * 16, 16), :] = a_ref[
                    pl.ds(s * 256 + nh * 128 + layer * 16, 16), :
                ]
        pool_ref[side, pl.ds(PLANE, PLANE), :] = ref[...].astype(f32)
        pool_ref[side, pl.ds(2 * PLANE, 32), :] = jnp.zeros((32, 128), f32)
    row = lax.broadcasted_iota(jnp.int32, (8, 128), 0)
    low = lane_low((8, 128))

    def one_slot(s, carry):
        def tile(a, b, c, n, l):
            nh, nl = n // 2, n % 2
            if (a, b, c) == (0, 0, 0):
                base = s * 256
            else:
                base = idx_ref[s, number_of[a, b, c]]
            if c == 0:
                return g_ref[pl.ds(pl.multiple_of(base + (nh * 128 + l * 16 + nl * 8), 8), 8), :]
            side = 0 if c < 0 else 1
            return pool_ref[side, pl.ds(pl.multiple_of(base + (nh * 16 + nl * 8), 8), 8), :]

        def pair(b, c, n, l):
            full = tile(0, b, c, n, l)
            after = tile(0, b, c, n + 1, l) if n < 3 else tile(1, b, c, 0, l)
            before = tile(0, b, c, n - 1, l) if n > 0 else tile(-1, b, c, 3, l)
            return full, jnp.where(low, after, before)

        for nh in range(2):
            for ll in range(10):
                c = -1 if ll == 0 else (1 if ll == 9 else 0)
                parts = [[] for _ in range(6)]
                for nl in range(2):
                    n = 2 * nh + nl
                    own = pair(0, c, n, ll - 1)
                    left = pair(-1, c, n, ll - 1)
                    right = pair(1, c, n, ll - 1)
                    for h in range(2):
                        parts[h].append(pltpu.roll(jnp.where(row == 7, left[h], own[h]), 1, 0))
                        parts[2 + h].append(own[h])
                        parts[4 + h].append(pltpu.roll(jnp.where(row == 0, right[h], own[h]), 7, 0))
                for q in range(6):
                    x_ref[s, nh, ll, :, q * 128 : (q + 1) * 128] = jnp.concatenate(
                        parts[q], axis=0
                    ).astype(bf16)
        return carry

    lax.fori_loop(0, CAP, one_slot, 0)


def convolve(x_ref, w_ref, epilogue):
    total = None
    for d in range(4):
        rows = jnp.concatenate([x_ref[:, :, d + 2 * m : d + 2 * m + 1] for m in range(4)], axis=2)
        term = jnp.dot(rows.reshape(512, 768), w_ref[d], preferred_element_type=f32)
        total = term if total is None else total + term
    for s in range(CAP):
        for nh in range(2):
            for l in range(E):
                at = (s * 8 + nh * 4 + l // 2) * 16
                lanes = (l % 2) * 128
                epilogue(pl.ds(s * 256 + nh * 128 + l * 16, 16), total[at : at + 16, lanes : lanes + 128])


def logistic(v):
    return 1.0 / (1.0 + jnp.exp(-v))


def conv1_kernel(idx_ref, a_ref, lo_ref, hi_ref, w_ref, x_ref, h_ref, slope_ref, up_ref, down_ref, g_ref, pool_ref):
    build(a_ref, lo_ref, hi_ref, idx_ref, g_ref, pool_ref, x_ref)

    def epilogue(rows, v):
        q = logistic(v)
        h_ref[rows, :] = a_ref[rows, :] + v * q
        slope_ref[rows, :] = q * (1.0 + v * (1.0 - q))

    convolve(x_ref, w_ref, epilogue)
    planes_out(h_ref, up_ref, down_ref)


def conv2_kernel(
    idx_ref, a_ref, lo_ref, hi_ref, w_ref, u_ref, x_ref, o_ref, e_ref, up_ref, down_ref, g_ref, pool_ref
):
    build(a_ref, lo_ref, hi_ref, idx_ref, g_ref, pool_ref, x_ref)

    def epilogue(rows, v):
        q = logistic(v)
        o_ref[rows, :] = a_ref[rows, :] + v * q
        e_ref[rows, :] = u_ref[rows, :] * (q * (1.0 + v * (1.0 - q)))

    convolve(x_ref, w_ref, epilogue)
    planes_out(e_ref, up_ref, down_ref)


def conv3_kernel(
    idx_ref, a_ref, lo_ref, hi_ref, w_ref, u_ref, slope_ref, hg_ref, e_ref, up_ref, down_ref, g_ref, pool_ref, x_ref
):
    build(a_ref, lo_ref, hi_ref, idx_ref, g_ref, pool_ref, x_ref)

    def epilogue(rows, v):
        grad = u_ref[rows, :] + v
        hg_ref[rows, :] = grad
        e_ref[rows, :] = grad * slope_ref[rows, :]

    convolve(x_ref, w_ref, epilogue)
    planes_out(e_ref, up_ref, down_ref)


def conv4_kernel(idx_ref, a_ref, lo_ref, hi_ref, w_ref, hg_ref, o_ref, g_ref, pool_ref, x_ref, r_ref, tmp_ref):
    build(a_ref, lo_ref, hi_ref, idx_ref, g_ref, pool_ref, x_ref)

    def epilogue(rows, v):
        r_ref[rows, :] = hg_ref[rows, :] + v

    convolve(x_ref, w_ref, epilogue)
    from_rows(r_ref, o_ref, tmp_ref)


def weight_grad(x_ref, e_ref, p_ref):
    low = lane_low((C, 128))
    errors = e_ref[...].T.astype(bf16)
    held = None
    for c in range(3):
        rows = x_ref[:, :, c : c + E].reshape(ROWS, 768)
        m = jnp.dot(errors, rows, preferred_element_type=f32)
        for b in range(3):
            number = 3 * c + b
            z0, z1 = m[:C, b * 256 : b * 256 + 128], m[C:, b * 256 : b * 256 + 128]
            y0, y1 = m[:C, b * 256 + 128 : (b + 1) * 256], m[C:, b * 256 + 128 : (b + 1) * 256]
            p_ref[pl.ds(number * C, C), :] = (z0 + pltpu.roll(jnp.where(low, y1, z1), C, 1)).astype(p_ref.dtype)
            if number % 2 == 0:
                held = z1 + pltpu.roll(y0, C, 1)
                if number == 8:
                    p_ref[pl.ds((9 + number // 2) * C, C), :] = jnp.where(low, held, 0.0).astype(p_ref.dtype)
            else:
                odd = pltpu.roll(z1, C, 1) + y0
                p_ref[pl.ds((9 + number // 2) * C, C), :] = jnp.where(low, held, odd).astype(p_ref.dtype)


def w2_kernel(x_ref, e_ref, r_ref, o_ref, p_ref, tmp_ref):
    from_rows(r_ref, o_ref, tmp_ref)
    weight_grad(x_ref, e_ref, p_ref)


def w1_kernel(x_ref, e_ref, second_ref, p_ref):
    p_ref[pl.ds(PACKED, PACKED), :] = second_ref[...]
    weight_grad(x_ref, e_ref, p_ref)


def finish_kernel(scale, r_ref, first_ref, second_ref):
    for which, ref in enumerate((first_ref, second_ref)):
        for c in range(3):
            for b in range(3):
                number = 3 * c + b
                k = 3 * b + c
                t = (r_ref[pl.ds(which * PACKED + number * C, C), :].astype(f32) * scale).T
                ref[9 + k] = t[:C]
                ref[18 + k] = t[C:]
                if number % 2 == 0:
                    t = (r_ref[pl.ds(which * PACKED + (9 + number // 2) * C, C), :].astype(f32) * scale).T
                    held = t[C:]
                    ref[k] = t[:C]
                else:
                    ref[k] = held


VMEM = pl.BlockSpec(memory_space=pltpu.VMEM)
SMEM = pl.BlockSpec(memory_space=pltpu.SMEM)
HBM = pl.BlockSpec(memory_space=pltpu.HBM)
FIELD = jax.ShapeDtypeStruct((ROWS, 128), f32)
PLANES = jax.ShapeDtypeStruct((PLANE, 128), bf16)
WINDOWS = (CAP, 2, 10, 16, 768)
WEIGHTS = jax.ShapeDtypeStruct((4, 768, 256), bf16)
CUBES = jax.ShapeDtypeStruct((1, CAP, C, E * E * E), f32)
POOLS = [pltpu.VMEM((ROWS + 256, 128), f32), pltpu.VMEM((2, 2 * PLANE + 32, 128), f32)]
TMP = pltpu.VMEM((16, C, 128), f32)


def call(kernel, scalars, arrays, outs, scratch=(), flops=0, place=VMEM):
    moved = sum(x.size * x.dtype.itemsize for x in arrays) + sum(o.size * o.dtype.itemsize for o in outs)
    return pl.pallas_call(
        kernel,
        out_shape=outs,
        in_specs=[SMEM] * len(scalars) + [place] * len(arrays),
        out_specs=[VMEM] * len(outs),
        scratch_shapes=list(scratch),
        cost_estimate=pl.CostEstimate(flops=flops, bytes_accessed=moved, transcendentals=0),
        compiler_params=pltpu.CompilerParams(vmem_limit_bytes=24 << 20),
    )(*scalars, *arrays)


def slot_table(neighbours):
    own = neighbours - lax.axis_index("brick") * CAP
    depth = jnp.array([item[2] for item in directions], jnp.int32)[None, :]
    inside = jnp.clip(own, 0, CAP - 1)
    below = jnp.where(own >= 0, inside, jnp.clip(own + 2 * CAP, CAP, 2 * CAP - 1))
    above = jnp.clip(own, 0, 2 * CAP - 1)
    present = neighbours >= 0
    middle = jnp.where(present, inside * 256, ROWS)
    outer = jnp.where(present, jnp.where(depth < 0, below, above) * 32, 2 * PLANE)
    return jnp.where(depth == 0, middle, outer).astype(jnp.int32)


def step(features, cotangent, first_kernel, second_kernel, counts, neighbours):
    bricks = lax.axis_size("brick")
    up_pairs = [(i, (i + 1) % bricks) for i in range(bricks)]
    down_pairs = [(j, i) for i, j in up_pairs]

    def exchange(up, down):
        return lax.ppermute(up, "brick", up_pairs), lax.ppermute(down, "brick", down_pairs)

    idx = slot_table(neighbours)
    windows = jax.ShapeDtypeStruct(WINDOWS, bf16)
    packed = jax.ShapeDtypeStruct((PACKED, 128), bf16)
    scratch_x = pltpu.VMEM(WINDOWS, bf16)
    work = 2 * ROWS * 2304 * 128

    inputs, up, down = call(pre_kernel, [counts], [features], [FIELD, PLANES, PLANES], [TMP])
    lo, hi = exchange(up, down)
    f1, f2, b1, b2, upstream = call(
        prep_kernel,
        [counts],
        [pltpu.with_memory_space_constraint(v, pltpu.HBM) for v in (first_kernel, second_kernel, cotangent)],
        [WEIGHTS] * 4 + [FIELD],
        [
            TMP,
            pltpu.VMEM((27, C, C), f32),
            pltpu.VMEM((27, C, C), f32),
            pltpu.VMEM((1, CAP, C, E * E * E), f32),
            pltpu.SemaphoreType.DMA((3,)),
        ],
        place=HBM,
    )
    x_in, hidden, slope1, up, down = call(
        conv1_kernel, [idx], [inputs, lo, hi, f1], [windows, FIELD, FIELD, PLANES, PLANES], POOLS, work
    )
    lo, hi = exchange(up, down)
    x_hidden, out_rows, second_err, up, down = call(
        conv2_kernel, [idx], [hidden, lo, hi, f2, upstream], [windows, FIELD, FIELD, PLANES, PLANES], POOLS, work
    )
    lo, hi = exchange(up, down)
    outputs, second_local = call(w2_kernel, [], [x_hidden, second_err, out_rows], [CUBES, packed], [TMP], work)
    hidden_grad, first_err, up, down = call(
        conv3_kernel,
        [idx],
        [second_err, lo, hi, b2, upstream, slope1],
        [FIELD, FIELD, PLANES, PLANES],
        POOLS + [scratch_x],
        work,
    )
    lo, hi = exchange(up, down)
    (partial,) = call(
        w1_kernel, [], [x_in, first_err, second_local], [jax.ShapeDtypeStruct((2 * PACKED, 128), bf16)], (), work
    )
    (input_grad,) = call(
        conv4_kernel,
        [idx],
        [first_err, lo, hi, b1, hidden_grad],
        [CUBES],
        POOLS + [scratch_x, pltpu.VMEM((ROWS, 128), f32), TMP],
        work,
    )
    axes = ("brick", "scene")
    scenes = lax.axis_size("scene")
    devices = bricks * scenes
    row = 4 if bricks % 4 == 0 else 1
    near, far = row * scenes, bricks // row
    near_groups = [list(range(z * near, (z + 1) * near)) for z in range(far)]
    far_groups = [[x + row * z for z in range(far)] for x in range(row)]
    share = 2 * PACKED // near

    def near_exchange(blocks):
        return lax.all_to_all(blocks, axes, 0, 0, axis_index_groups=near_groups, tiled=True)

    def far_exchange(blocks):
        return lax.all_to_all(blocks, "brick", 0, 0, axis_index_groups=far_groups, tiled=True)

    def total_of(blocks):
        return jnp.sum(blocks.astype(f32), axis=0).astype(bf16)

    def spread(block, count):
        return jnp.broadcast_to(block[None], (count,) + block.shape)

    mine = total_of(near_exchange(partial.reshape(near, share, 128)))
    mine = total_of(far_exchange(spread(mine, far)))
    total = near_exchange(spread(mine, near))
    scale = float((devices * CAP * E * E * E) ** -0.5)
    grads = jax.ShapeDtypeStruct((27, C, C), f32)
    first_grad, second_grad = call(
        lambda *refs: finish_kernel(scale, *refs), [], [total.reshape(2 * PACKED, 128)], [grads, grads]
    )
    return (outputs, input_grad, first_grad, second_grad)


def solution(mesh):
    return jax.shard_map(
        step,
        mesh=mesh,
        in_specs=(
            P("scene", "brick", None, None),
            P("scene", "brick", None, None),
            P(),
            P(),
            P("brick"),
            P("brick", None),
        ),
        out_specs=(P("scene", "brick", None, None), P("scene", "brick", None, None), P(), P()),
        check_vma=False,
    )
```

```python
import functools

import jax
import jax.numpy as jnp
from jax import lax
from jax.experimental import pallas as pl
from jax.experimental.pallas import tpu as pltpu
from jax.sharding import PartitionSpec as P


E = 8
C = 64
CAP = 4
f32 = jnp.float32
bf16 = jnp.bfloat16
offsets = [(a, b, c) for a in (-1, 0, 1) for b in (-1, 0, 1) for c in (-1, 0, 1)]
directions = [item for item in offsets if item != (0, 0, 0)]
number_of = {item: n for n, item in enumerate(directions)}

ROWS = CAP * 256
PLANE = CAP * 32
PACKED = 896


def row0(s, n, l):
    return s * 256 + (n // 2) * 128 + l * 16 + (n % 2) * 8


def flip(t):
    tt = t.T
    return jnp.concatenate([tt[:C], tt[C:]], axis=1)


def lane_low(shape):
    return lax.broadcasted_iota(jnp.int32, shape, 1) < C


def to_rows(x_ref, a_ref, tmp_ref, counts_ref, slots=range(CAP)):
    for s in slots:
        occupied = jnp.where(s < counts_ref[0], 1.0, 0.0).astype(f32)
        for n in range(4):
            t = x_ref[0, s, :, n * 128 : (n + 1) * 128] * occupied
            tmp_ref[s * 4 + n] = flip(t)
            for l in range(E):
                a_ref[pl.ds(row0(s, n, l), 8), :] = tmp_ref[s * 4 + n, pl.ds(l, 8, stride=8), :]


def from_rows(a_ref, o_ref, tmp_ref):
    for s in range(CAP):
        for n in range(4):
            for l in range(E):
                tmp_ref[s * 4 + n, pl.ds(l, 8, stride=8), :] = a_ref[pl.ds(row0(s, n, l), 8), :]
            o_ref[0, s, :, n * 128 : (n + 1) * 128] = flip(tmp_ref[s * 4 + n])


def planes_out(a_ref, up_ref, down_ref):
    for s in range(CAP):
        for nh in range(2):
            base = s * 256 + nh * 128
            to = pl.ds(s * 32 + nh * 16, 16)
            up_ref[to, :] = a_ref[pl.ds(base + 7 * 16, 16), :].astype(bf16)
            down_ref[to, :] = a_ref[pl.ds(base, 16), :].astype(bf16)


def pre_kernel(counts_ref, x_hbm, a_ref, up_ref, down_ref, tmp_ref, x_ref, sems):
    copies = [pltpu.make_async_copy(x_hbm.at[0, s], x_ref.at[0, s], sems.at[s]) for s in range(CAP)]
    for copy in copies:
        copy.start()
    for s in range(CAP):
        copies[s].wait()
        to_rows(x_ref, a_ref, tmp_ref, counts_ref, (s,))
    planes_out(a_ref, up_ref, down_ref)


def flat_weights(w_ref, o_ref, back):
    zero = jnp.zeros((C, C), f32)

    def block(a, b, c):
        k = 9 * (a + 1) + 3 * (b + 1) + (c + 1)
        return w_ref[26 - k].T if back else w_ref[k]

    blank = jnp.zeros((256, 128), bf16)
    for bi, b in enumerate((-1, 0, 1)):
        rows = pl.ds(bi * 256, 256)
        o_ref[0, rows, 128:] = blank
        o_ref[3, rows, :128] = blank
        for ci, c in enumerate((-1, 0, 1)):
            low, mid, high = (block(a, b, c) for a in (-1, 0, 1))
            left = jnp.concatenate([mid, high, zero, low], axis=0)
            right = jnp.concatenate([low, mid, high, zero], axis=0)
            joined = jnp.concatenate([left, right], axis=1).astype(bf16)
            o_ref[ci, rows, :128] = joined
            o_ref[ci + 1, rows, 128:] = joined


def prep1_kernel(w1_hbm, f1_ref, w1_ref, sem):
    copy = pltpu.make_async_copy(w1_hbm, w1_ref, sem)
    copy.start()
    copy.wait()
    flat_weights(w1_ref, f1_ref, False)


def prep2_kernel(counts_ref, w1_hbm, w2_hbm, x_hbm, f2_ref, b1_ref, b2_ref, u_ref, tmp_ref, w1_ref, w2_ref, x_ref, sems):
    pairs = ((w2_hbm, w2_ref), (w1_hbm, w1_ref), (x_hbm, x_ref))
    copies = [pltpu.make_async_copy(src, dst, sems.at[n]) for n, (src, dst) in enumerate(pairs)]
    for copy in copies:
        copy.start()
    copies[0].wait()
    flat_weights(w2_ref, f2_ref, False)
    flat_weights(w2_ref, b2_ref, True)
    copies[1].wait()
    flat_weights(w1_ref, b1_ref, True)
    copies[2].wait()
    to_rows(x_ref, u_ref, tmp_ref, counts_ref)


def build(idx_ref, source, x_ref, layers, c):
    row = lax.broadcasted_iota(jnp.int32, (8, 128), 0)
    low = lane_low((8, 128))

    def one_slot(s, carry):
        def tile(a, b, n, l):
            base = s * 256 if (a, b, c) == (0, 0, 0) else idx_ref[s, number_of[a, b, c]]
            return source(base, n, l)

        def pair(b, n, l):
            full = tile(0, b, n, l)
            after = tile(0, b, n + 1, l) if n < 3 else tile(1, b, 0, l)
            before = tile(0, b, n - 1, l) if n > 0 else tile(-1, b, 3, l)
            return full, jnp.where(low, after, before)

        for nh in range(2):
            for at, l in layers:
                parts = [[] for _ in range(6)]
                for nl in range(2):
                    n = 2 * nh + nl
                    own, left, right = pair(0, n, l), pair(-1, n, l), pair(1, n, l)
                    for h in range(2):
                        parts[h].append(pltpu.roll(jnp.where(row == 7, left[h], own[h]), 1, 0))
                        parts[2 + h].append(own[h])
                        parts[4 + h].append(pltpu.roll(jnp.where(row == 0, right[h], own[h]), 7, 0))
                for q in range(6):
                    x_ref[s, nh, at, :, q * 128 : (q + 1) * 128] = jnp.concatenate(parts[q], axis=0).astype(bf16)
        return carry

    lax.fori_loop(0, CAP, one_slot, 0)


def build_center(idx_ref, a_ref, g_ref, xc_ref):
    g_ref[pl.ds(0, ROWS), :] = a_ref[...]
    g_ref[pl.ds(ROWS, 256), :] = jnp.zeros((256, 128), f32)

    def source(base, n, l):
        return g_ref[pl.ds(pl.multiple_of(base + ((n // 2) * 128 + l * 16 + (n % 2) * 8), 8), 8), :]

    build(idx_ref, source, xc_ref, [(l, l) for l in range(E)], 0)


def build_outer(idx_ref, a_ref, lo_ref, hi_ref, pool_ref, xo_ref):
    for side, (ref, layer) in enumerate(((lo_ref, 7), (hi_ref, 0))):
        for s in range(CAP):
            for nh in range(2):
                pool_ref[side, pl.ds(s * 32 + nh * 16, 16), :] = a_ref[
                    pl.ds(s * 256 + nh * 128 + layer * 16, 16), :
                ]
        pool_ref[side, pl.ds(PLANE, PLANE), :] = ref[...].astype(f32)
        pool_ref[side, pl.ds(2 * PLANE, 32), :] = jnp.zeros((32, 128), f32)

        def source(base, n, l, side=side):
            return pool_ref[side, pl.ds(pl.multiple_of(base + ((n // 2) * 16 + (n % 2) * 8), 8), 8), :]

        build(idx_ref, source, xo_ref, [(side, 0)], -1 if side == 0 else 1)


def layers_of(xc_ref, xo_ref, first, count):
    parts = []
    if first == 0:
        parts.append(xo_ref[:, :, 0:1])
    low, high = max(first, 1), min(first + count, 9)
    if high > low:
        parts.append(xc_ref[:, :, low - 1 : high - 1])
    if first + count == 10:
        parts.append(xo_ref[:, :, 1:2])
    return parts[0] if len(parts) == 1 else jnp.concatenate(parts, axis=2)


def convolve(xc_ref, xo_ref, w_ref, pairs, epilogue):
    total = None
    count = len(pairs)
    for d in range(4):
        rows = jnp.concatenate([layers_of(xc_ref, xo_ref, d + 2 * m, 1) for m in pairs], axis=2)
        term = jnp.dot(rows.reshape(128 * count, 768), w_ref[d], preferred_element_type=f32)
        total = term if total is None else total + term
    for s in range(CAP):
        for nh in range(2):
            for i, m in enumerate(pairs):
                for h in range(2):
                    at = ((s * 2 + nh) * count + i) * 16
                    epilogue(s, nh, 2 * m + h, total[at : at + 16, h * 128 : h * 128 + 128])


CENTER = (1, 2)
OUTER = (0, 3)
ALL = (0, 1, 2, 3)


def full_rows(s, nh, l):
    return pl.ds(s * 256 + nh * 128 + l * 16, 16)


def center_rows(s, nh, l):
    return pl.ds((s * 2 + nh) * 64 + (l - 2) * 16, 16)


def take_center(part_ref, full_ref):
    for s in range(CAP):
        for nh in range(2):
            full_ref[pl.ds(s * 256 + nh * 128 + 32, 64), :] = part_ref[pl.ds((s * 2 + nh) * 64, 64), :]


def logistic(v):
    return 1.0 / (1.0 + jnp.exp(-v))


def first_layer(a, v):
    q = logistic(v)
    return a + v * q, q * (1.0 + v * (1.0 - q))


def second_layer(a, v, u):
    q = logistic(v)
    return a + v * q, u * (q * (1.0 + v * (1.0 - q)))


def second_back(v, u, slope):
    grad = u + v
    return grad, grad * slope


def center_kernel(formula, count, idx_ref, a_ref, w_ref, *refs):
    extra, (xc_ref, p_ref, q_ref, g_ref) = refs[:count], refs[count:]
    build_center(idx_ref, a_ref, g_ref, xc_ref)

    def epilogue(s, nh, l, v):
        full, part = full_rows(s, nh, l), center_rows(s, nh, l)
        p_ref[part, :], q_ref[part, :] = formula(v, a_ref[full, :], *[r[full, :] for r in extra])

    convolve(xc_ref, None, w_ref, CENTER, epilogue)


def outer_kernel(formula, count, send, idx_ref, a_ref, w_ref, lo_ref, hi_ref, xc_ref, pc_ref, qc_ref, *refs):
    extra, (xo_ref, p_ref, q_ref, up_ref, down_ref, pool_ref) = refs[:count], refs[count:]
    build_outer(idx_ref, a_ref, lo_ref, hi_ref, pool_ref, xo_ref)

    def epilogue(s, nh, l, v):
        full = full_rows(s, nh, l)
        p_ref[full, :], q_ref[full, :] = formula(v, a_ref[full, :], *[r[full, :] for r in extra])

    convolve(xc_ref, xo_ref, w_ref, OUTER, epilogue)
    planes_out((p_ref, q_ref)[send], up_ref, down_ref)
    take_center(pc_ref, p_ref)
    take_center(qc_ref, q_ref)


def last_kernel(idx_ref, a_ref, lo_ref, hi_ref, w_ref, hg_ref, o_ref, g_ref, pool_ref, xc_ref, xo_ref, r_ref, tmp_ref):
    build_center(idx_ref, a_ref, g_ref, xc_ref)
    build_outer(idx_ref, a_ref, lo_ref, hi_ref, pool_ref, xo_ref)

    def epilogue(s, nh, l, v):
        full = full_rows(s, nh, l)
        r_ref[full, :] = hg_ref[full, :] + v

    convolve(xc_ref, xo_ref, w_ref, ALL, epilogue)
    from_rows(r_ref, o_ref, tmp_ref)


def rows_kernel(r_ref, o_ref, tmp_ref):
    from_rows(r_ref, o_ref, tmp_ref)


def weight_grad(xc_ref, xo_ref, e_ref, p_ref):
    low = lane_low((C, 128))
    errors = e_ref[...].T.astype(bf16)
    held = None
    for c in range(3):
        rows = layers_of(xc_ref, xo_ref, c, E).reshape(ROWS, 768)
        m = jnp.dot(errors, rows, preferred_element_type=f32)
        for b in range(3):
            number = 3 * c + b
            z0, z1 = m[:C, b * 256 : b * 256 + 128], m[C:, b * 256 : b * 256 + 128]
            y0, y1 = m[:C, b * 256 + 128 : (b + 1) * 256], m[C:, b * 256 + 128 : (b + 1) * 256]
            p_ref[pl.ds(number * C, C), :] = (z0 + pltpu.roll(jnp.where(low, y1, z1), C, 1)).astype(p_ref.dtype)
            if number % 2 == 0:
                held = z1 + pltpu.roll(y0, C, 1)
                if number == 8:
                    p_ref[pl.ds((9 + number // 2) * C, C), :] = jnp.where(low, held, 0.0).astype(p_ref.dtype)
            else:
                odd = pltpu.roll(z1, C, 1) + y0
                p_ref[pl.ds((9 + number // 2) * C, C), :] = jnp.where(low, held, odd).astype(p_ref.dtype)


def w2_kernel(xc_ref, xo_ref, e_ref, p_ref):
    weight_grad(xc_ref, xo_ref, e_ref, p_ref)


def w1_kernel(xc_ref, xo_ref, e_ref, second_ref, p_ref):
    p_ref[pl.ds(PACKED, PACKED), :] = second_ref[...]
    weight_grad(xc_ref, xo_ref, e_ref, p_ref)


def finish_kernel(scale, r_ref, first_hbm, second_hbm, first_ref, second_ref, sems):
    copies = []
    for which, (ref, hbm) in enumerate(((first_ref, first_hbm), (second_ref, second_hbm))):
        for c in range(3):
            for b in range(3):
                number = 3 * c + b
                k = 3 * b + c
                t = (r_ref[pl.ds(which * PACKED + number * C, C), :].astype(f32) * scale).T
                ref[9 + k] = t[:C]
                ref[18 + k] = t[C:]
                if number % 2 == 0:
                    t = (r_ref[pl.ds(which * PACKED + (9 + number // 2) * C, C), :].astype(f32) * scale).T
                    held = t[C:]
                    ref[k] = t[:C]
                else:
                    ref[k] = held
        copy = pltpu.make_async_copy(ref, hbm, sems.at[which])
        copy.start()
        copies.append(copy)
    for copy in copies:
        copy.wait()


VMEM = pl.BlockSpec(memory_space=pltpu.VMEM)
SMEM = pl.BlockSpec(memory_space=pltpu.SMEM)
HBM = pl.BlockSpec(memory_space=pltpu.HBM)
FIELD = jax.ShapeDtypeStruct((ROWS, 128), f32)
PLANES = jax.ShapeDtypeStruct((PLANE, 128), bf16)
CENTERS = (CAP, 2, 8, 16, 768)
OUTERS = (CAP, 2, 2, 16, 768)
HALF = jax.ShapeDtypeStruct((ROWS // 2, 128), f32)
GRADS = jax.ShapeDtypeStruct((27, C, C), f32)
WEIGHTS = jax.ShapeDtypeStruct((4, 768, 256), bf16)
CUBES = jax.ShapeDtypeStruct((1, CAP, C, E * E * E), f32)
OWN = pltpu.VMEM((ROWS + 256, 128), f32)
POOL = pltpu.VMEM((2, 2 * PLANE + 32, 128), f32)
TMP = pltpu.VMEM((16, C, 128), f32)


def call(kernel, scalars, arrays, outs, scratch=(), flops=0, place=VMEM, result=VMEM):
    moved = sum(x.size * x.dtype.itemsize for x in arrays) + sum(o.size * o.dtype.itemsize for o in outs)
    return pl.pallas_call(
        kernel,
        out_shape=outs,
        in_specs=[SMEM] * len(scalars) + [place] * len(arrays),
        out_specs=[result] * len(outs),
        scratch_shapes=list(scratch),
        cost_estimate=pl.CostEstimate(flops=flops, bytes_accessed=moved, transcendentals=0),
        compiler_params=pltpu.CompilerParams(vmem_limit_bytes=24 << 20),
    )(*scalars, *arrays)


def slot_table(neighbours):
    own = neighbours - lax.axis_index("brick") * CAP
    depth = jnp.array([item[2] for item in directions], jnp.int32)[None, :]
    inside = jnp.clip(own, 0, CAP - 1)
    below = jnp.where(own >= 0, inside, jnp.clip(own + 2 * CAP, CAP, 2 * CAP - 1))
    above = jnp.clip(own, 0, 2 * CAP - 1)
    present = neighbours >= 0
    middle = jnp.where(present, inside * 256, ROWS)
    outer = jnp.where(present, jnp.where(depth < 0, below, above) * 32, 2 * PLANE)
    return jnp.where(depth == 0, middle, outer).astype(jnp.int32)


def step(features, cotangent, first_kernel, second_kernel, counts, neighbours):
    bricks = lax.axis_size("brick")
    up_pairs = [(i, (i + 1) % bricks) for i in range(bricks)]
    down_pairs = [(j, i) for i, j in up_pairs]

    def exchange(up, down):
        return lax.ppermute(up, "brick", up_pairs), lax.ppermute(down, "brick", down_pairs)

    idx = slot_table(neighbours)
    centers = jax.ShapeDtypeStruct(CENTERS, bf16)
    outers = jax.ShapeDtypeStruct(OUTERS, bf16)
    packed = jax.ShapeDtypeStruct((PACKED, 128), bf16)
    raw = pltpu.VMEM((27, C, C), f32)
    cubes = pltpu.VMEM((1, CAP, C, E * E * E), f32)
    work = 2 * ROWS * 2304 * 128
    features, cotangent, first_kernel, second_kernel = [
        pltpu.with_memory_space_constraint(v, pltpu.HBM) for v in (features, cotangent, first_kernel, second_kernel)
    ]

    def layer(formula, send, field, weights, extra, between):
        planes = between
        xc, pc, qc = call(
            functools.partial(center_kernel, formula, len(extra)),
            [idx],
            [field, weights] + extra,
            [centers, HALF, HALF],
            [OWN],
            work // 2,
        )
        xo, p, q, up, down = call(
            functools.partial(outer_kernel, formula, len(extra), send),
            [idx],
            [field, weights, *planes, xc, pc, qc] + extra,
            [outers, FIELD, FIELD, PLANES, PLANES],
            [POOL],
            work // 2,
        )
        return xc, xo, p, q, up, down

    inputs, up, down = call(
        pre_kernel,
        [counts],
        [features],
        [FIELD, PLANES, PLANES],
        [TMP, cubes, pltpu.SemaphoreType.DMA((CAP,))],
        place=HBM,
    )
    planes = exchange(up, down)
    (f1,) = call(prep1_kernel, [], [first_kernel], [WEIGHTS], [raw, pltpu.SemaphoreType.DMA], place=HBM)
    xc1, xo1, hidden, slope1, up, down = layer(lambda v, a: first_layer(a, v), 0, inputs, f1, [], planes)
    planes = exchange(up, down)
    f2, b1, b2, upstream = call(
        prep2_kernel,
        [counts],
        [first_kernel, second_kernel, cotangent],
        [WEIGHTS] * 3 + [FIELD],
        [TMP, raw, raw, cubes, pltpu.SemaphoreType.DMA((3,))],
        place=HBM,
    )
    xc2, xo2, out_rows, second_err, up, down = layer(
        lambda v, a, u: second_layer(a, v, u), 1, hidden, f2, [upstream], planes
    )
    planes = exchange(up, down)
    (second_local,) = call(w2_kernel, [], [xc2, xo2, second_err], [packed], (), work)
    _, _, hidden_grad, first_err, up, down = layer(
        lambda v, a, u, slope: second_back(v, u, slope), 1, second_err, b2, [upstream, slope1], planes
    )
    lo, hi = exchange(up, down)
    (partial,) = call(
        w1_kernel, [], [xc1, xo1, first_err, second_local], [jax.ShapeDtypeStruct((2 * PACKED, 128), bf16)], (), work
    )
    (input_grad,) = call(
        last_kernel,
        [idx],
        [first_err, lo, hi, b1, hidden_grad],
        [CUBES],
        [OWN, POOL, pltpu.VMEM(CENTERS, bf16), pltpu.VMEM(OUTERS, bf16), pltpu.VMEM((ROWS, 128), f32), TMP],
        work,
    )
    (outputs,) = call(rows_kernel, [], [out_rows], [CUBES], [TMP])
    axes = ("brick", "scene")
    scenes = lax.axis_size("scene")
    devices = bricks * scenes
    row = 4 if bricks % 4 == 0 else 1
    near, far = row * scenes, bricks // row
    near_groups = [list(range(z * near, (z + 1) * near)) for z in range(far)]
    far_groups = [[x + row * z for z in range(far)] for x in range(row)]
    share = 2 * PACKED // near

    def near_exchange(blocks):
        return lax.all_to_all(blocks, axes, 0, 0, axis_index_groups=near_groups, tiled=True)

    def far_exchange(blocks):
        return lax.all_to_all(blocks, "brick", 0, 0, axis_index_groups=far_groups, tiled=True)

    def total_of(blocks):
        return jnp.sum(blocks.astype(f32), axis=0).astype(bf16)

    def spread(block, count):
        return jnp.broadcast_to(block[None], (count,) + block.shape)

    scattered = near_exchange(partial.reshape(near, share, 128))
    mine = total_of(scattered)
    mine = total_of(far_exchange(spread(mine, far)))
    total = near_exchange(spread(mine, near))
    scale = float((devices * CAP * E * E * E) ** -0.5)
    first_grad, second_grad = call(
        functools.partial(finish_kernel, scale),
        [],
        [total.reshape(2 * PACKED, 128)],
        [GRADS, GRADS],
        [raw, raw, pltpu.SemaphoreType.DMA((2,))],
        result=HBM,
    )
    return (outputs, input_grad, first_grad, second_grad)


def solution(mesh):
    return jax.shard_map(
        step,
        mesh=mesh,
        in_specs=(
            P("scene", "brick", None, None),
            P("scene", "brick", None, None),
            P(),
            P(),
            P("brick"),
            P("brick", None),
        ),
        out_specs=(P("scene", "brick", None, None), P("scene", "brick", None, None), P(), P()),
        check_vma=False,
    )
```

```python
import functools

import jax
import jax.numpy as jnp
from jax import lax
from jax.experimental import pallas as pl
from jax.experimental.pallas import tpu as pltpu
from jax.sharding import PartitionSpec as P


E = 8
C = 64
CAP = 4
f32 = jnp.float32
bf16 = jnp.bfloat16
offsets = [(a, b, c) for a in (-1, 0, 1) for b in (-1, 0, 1) for c in (-1, 0, 1)]
directions = [item for item in offsets if item != (0, 0, 0)]
number_of = {item: n for n, item in enumerate(directions)}

ROWS = CAP * 256
PLANE = CAP * 32
PACKED = 896


def row0(s, n, l):
    return s * 256 + (n // 2) * 128 + l * 16 + (n % 2) * 8


def flip(t):
    tt = t.T
    return jnp.concatenate([tt[:C], tt[C:]], axis=1)


def lane_low(shape):
    return lax.broadcasted_iota(jnp.int32, shape, 1) < C


def to_rows(x_ref, a_ref, tmp_ref, counts_ref):
    for s in range(CAP):
        occupied = jnp.where(s < counts_ref[0], 1.0, 0.0).astype(f32)
        for n in range(4):
            t = x_ref[0, s, :, n * 128 : (n + 1) * 128] * occupied
            tmp_ref[s * 4 + n] = flip(t)
            for l in range(E):
                a_ref[pl.ds(row0(s, n, l), 8), :] = tmp_ref[s * 4 + n, pl.ds(l, 8, stride=8), :]


def from_rows(a_ref, o_ref, tmp_ref):
    for s in range(CAP):
        for n in range(4):
            for l in range(E):
                tmp_ref[s * 4 + n, pl.ds(l, 8, stride=8), :] = a_ref[pl.ds(row0(s, n, l), 8), :]
            o_ref[0, s, :, n * 128 : (n + 1) * 128] = flip(tmp_ref[s * 4 + n])


def planes_out(a_ref, up_ref, down_ref):
    for s in range(CAP):
        for nh in range(2):
            base = s * 256 + nh * 128
            to = pl.ds(s * 32 + nh * 16, 16)
            up_ref[to, :] = a_ref[pl.ds(base + 7 * 16, 16), :].astype(bf16)
            down_ref[to, :] = a_ref[pl.ds(base, 16), :].astype(bf16)


def pre_kernel(
    counts_ref, x_hbm, w1_hbm, u_hbm, w2_hbm, a_ref, up_ref, down_ref, w1_ref, u_ref, w2_ref, tmp_ref, x_ref, sems
):
    pairs = ((x_hbm, x_ref), (w1_hbm, w1_ref), (w2_hbm, w2_ref), (u_hbm, u_ref))
    copies = [pltpu.make_async_copy(src, dst, sems.at[n]) for n, (src, dst) in enumerate(pairs)]
    for copy in copies:
        copy.start()
    copies[0].wait()
    to_rows(x_ref, a_ref, tmp_ref, counts_ref)
    planes_out(a_ref, up_ref, down_ref)
    for copy in copies[1:]:
        copy.wait()


def flat_weights(w_ref, o_ref, back):
    zero = jnp.zeros((C, C), f32)

    def block(a, b, c):
        k = 9 * (a + 1) + 3 * (b + 1) + (c + 1)
        return w_ref[26 - k].T if back else w_ref[k]

    blank = jnp.zeros((256, 128), bf16)
    for bi, b in enumerate((-1, 0, 1)):
        rows = pl.ds(bi * 256, 256)
        o_ref[0, rows, 128:] = blank
        o_ref[3, rows, :128] = blank
        for ci, c in enumerate((-1, 0, 1)):
            low, mid, high = (block(a, b, c) for a in (-1, 0, 1))
            left = jnp.concatenate([mid, high, zero, low], axis=0)
            right = jnp.concatenate([low, mid, high, zero], axis=0)
            joined = jnp.concatenate([left, right], axis=1).astype(bf16)
            o_ref[ci, rows, :128] = joined
            o_ref[ci + 1, rows, 128:] = joined


def prep1_kernel(w1_ref, f1_ref):
    flat_weights(w1_ref, f1_ref, False)


def prep2_kernel(counts_ref, w2_ref, x_ref, f2_ref, u_ref, tmp_ref):
    flat_weights(w2_ref, f2_ref, False)
    to_rows(x_ref, u_ref, tmp_ref, counts_ref)


def back_kernel(w_ref, b_ref):
    flat_weights(w_ref, b_ref, True)


def build(idx_ref, source, x_ref, layers, c):
    row = lax.broadcasted_iota(jnp.int32, (8, 128), 0)
    low = lane_low((8, 128))

    def one_slot(s, carry):
        def tile(a, b, n, l):
            base = s * 256 if (a, b, c) == (0, 0, 0) else idx_ref[s, number_of[a, b, c]]
            return source(base, n, l)

        def pair(b, n, l):
            full = tile(0, b, n, l)
            after = tile(0, b, n + 1, l) if n < 3 else tile(1, b, 0, l)
            before = tile(0, b, n - 1, l) if n > 0 else tile(-1, b, 3, l)
            return full, jnp.where(low, after, before)

        for nh in range(2):
            for at, l in layers:
                parts = [[] for _ in range(6)]
                for nl in range(2):
                    n = 2 * nh + nl
                    own, left, right = pair(0, n, l), pair(-1, n, l), pair(1, n, l)
                    for h in range(2):
                        parts[h].append(pltpu.roll(jnp.where(row == 7, left[h], own[h]), 1, 0))
                        parts[2 + h].append(own[h])
                        parts[4 + h].append(pltpu.roll(jnp.where(row == 0, right[h], own[h]), 7, 0))
                for q in range(6):
                    x_ref[s, nh, at, :, q * 128 : (q + 1) * 128] = jnp.concatenate(parts[q], axis=0).astype(bf16)
        return carry

    lax.fori_loop(0, CAP, one_slot, 0)


def build_center(idx_ref, a_ref, g_ref, xc_ref):
    g_ref[pl.ds(0, ROWS), :] = a_ref[...]
    g_ref[pl.ds(ROWS, 256), :] = jnp.zeros((256, 128), f32)

    def source(base, n, l):
        return g_ref[pl.ds(pl.multiple_of(base + ((n // 2) * 128 + l * 16 + (n % 2) * 8), 8), 8), :]

    build(idx_ref, source, xc_ref, [(l, l) for l in range(E)], 0)


def build_outer(idx_ref, a_ref, lo_ref, hi_ref, pool_ref, xo_ref):
    for side, (ref, layer) in enumerate(((lo_ref, 7), (hi_ref, 0))):
        for s in range(CAP):
            for nh in range(2):
                pool_ref[side, pl.ds(s * 32 + nh * 16, 16), :] = a_ref[
                    pl.ds(s * 256 + nh * 128 + layer * 16, 16), :
                ]
        pool_ref[side, pl.ds(PLANE, PLANE), :] = ref[...].astype(f32)
        pool_ref[side, pl.ds(2 * PLANE, 32), :] = jnp.zeros((32, 128), f32)

        def source(base, n, l, side=side):
            return pool_ref[side, pl.ds(pl.multiple_of(base + ((n // 2) * 16 + (n % 2) * 8), 8), 8), :]

        build(idx_ref, source, xo_ref, [(side, 0)], -1 if side == 0 else 1)


def layers_of(xc_ref, xo_ref, first, count):
    parts = []
    if first == 0:
        parts.append(xo_ref[:, :, 0:1])
    low, high = max(first, 1), min(first + count, 9)
    if high > low:
        parts.append(xc_ref[:, :, low - 1 : high - 1])
    if first + count == 10:
        parts.append(xo_ref[:, :, 1:2])
    return parts[0] if len(parts) == 1 else jnp.concatenate(parts, axis=2)


def convolve(xc_ref, xo_ref, w_ref, pairs, epilogue):
    total = None
    count = len(pairs)
    for d in range(4):
        rows = jnp.concatenate([layers_of(xc_ref, xo_ref, d + 2 * m, 1) for m in pairs], axis=2)
        term = jnp.dot(rows.reshape(128 * count, 768), w_ref[d], preferred_element_type=f32)
        total = term if total is None else total + term
    for s in range(CAP):
        for nh in range(2):
            for i, m in enumerate(pairs):
                for h in range(2):
                    at = ((s * 2 + nh) * count + i) * 16
                    epilogue(s, nh, 2 * m + h, total[at : at + 16, h * 128 : h * 128 + 128])


CENTER = (1, 2)
OUTER = (0, 3)
ALL = (0, 1, 2, 3)


def full_rows(s, nh, l):
    return pl.ds(s * 256 + nh * 128 + l * 16, 16)


def center_rows(s, nh, l):
    return pl.ds((s * 2 + nh) * 64 + (l - 2) * 16, 16)


def take_center(part_ref, full_ref):
    for s in range(CAP):
        for nh in range(2):
            full_ref[pl.ds(s * 256 + nh * 128 + 32, 64), :] = part_ref[pl.ds((s * 2 + nh) * 64, 64), :]


def logistic(v):
    return 1.0 / (1.0 + jnp.exp(-v))


def first_layer(a, v):
    q = logistic(v)
    return a + v * q, q * (1.0 + v * (1.0 - q))


def second_layer(a, v, u):
    q = logistic(v)
    return a + v * q, u * (q * (1.0 + v * (1.0 - q)))


def second_back(v, u, slope):
    grad = u + v
    return grad, grad * slope


def center_kernel(formula, count, idx_ref, a_ref, w_ref, *refs):
    extra, (xc_ref, p_ref, q_ref, g_ref) = refs[:count], refs[count:]
    build_center(idx_ref, a_ref, g_ref, xc_ref)

    def epilogue(s, nh, l, v):
        full, part = full_rows(s, nh, l), center_rows(s, nh, l)
        p_ref[part, :], q_ref[part, :] = formula(v, a_ref[full, :], *[r[full, :] for r in extra])

    convolve(xc_ref, None, w_ref, CENTER, epilogue)


def outer_kernel(formula, count, send, idx_ref, a_ref, w_ref, lo_ref, hi_ref, xc_ref, pc_ref, qc_ref, *refs):
    extra, (p_ref, q_ref, up_ref, down_ref, xo_ref, pool_ref) = refs[:count], refs[count:]
    build_outer(idx_ref, a_ref, lo_ref, hi_ref, pool_ref, xo_ref)

    def epilogue(s, nh, l, v):
        full = full_rows(s, nh, l)
        p_ref[full, :], q_ref[full, :] = formula(v, a_ref[full, :], *[r[full, :] for r in extra])

    convolve(xc_ref, xo_ref, w_ref, OUTER, epilogue)
    planes_out((p_ref, q_ref)[send], up_ref, down_ref)
    take_center(pc_ref, p_ref)
    take_center(qc_ref, q_ref)


def last_kernel(idx_ref, a_ref, lo_ref, hi_ref, w_ref, hg_ref, o_ref, g_ref, pool_ref, xc_ref, xo_ref, r_ref, tmp_ref):
    build_center(idx_ref, a_ref, g_ref, xc_ref)
    build_outer(idx_ref, a_ref, lo_ref, hi_ref, pool_ref, xo_ref)

    def epilogue(s, nh, l, v):
        full = full_rows(s, nh, l)
        r_ref[full, :] = hg_ref[full, :] + v

    convolve(xc_ref, xo_ref, w_ref, ALL, epilogue)
    from_rows(r_ref, o_ref, tmp_ref)


def rows_kernel(r_ref, o_ref, tmp_ref):
    from_rows(r_ref, o_ref, tmp_ref)


def weight_grad(xc_ref, xo_ref, e_ref, p_ref, ready=None):
    low = lane_low((C, 128))
    errors = e_ref[...].T.astype(bf16)
    held = None
    for c in range(3):
        rows = layers_of(xc_ref, xo_ref, c, E).reshape(ROWS, 768)
        m = jnp.dot(errors, rows, preferred_element_type=f32)
        for b in range(3):
            number = 3 * c + b
            z0, z1 = m[:C, b * 256 : b * 256 + 128], m[C:, b * 256 : b * 256 + 128]
            y0, y1 = m[:C, b * 256 + 128 : (b + 1) * 256], m[C:, b * 256 + 128 : (b + 1) * 256]
            p_ref[pl.ds(number * C, C), :] = (z0 + pltpu.roll(jnp.where(low, y1, z1), C, 1)).astype(p_ref.dtype)
            if number % 2 == 0:
                held = z1 + pltpu.roll(y0, C, 1)
                if number == 8:
                    p_ref[pl.ds((9 + number // 2) * C, C), :] = jnp.where(low, held, 0.0).astype(p_ref.dtype)
            else:
                odd = pltpu.roll(z1, C, 1) + y0
                p_ref[pl.ds((9 + number // 2) * C, C), :] = jnp.where(low, held, odd).astype(p_ref.dtype)
        if ready is not None:
            ready(c)


def w2_kernel(xc_ref, xo_ref, e_ref, p_ref):
    weight_grad(xc_ref, xo_ref, e_ref, p_ref)


def w1_kernel(xc_ref, xo_ref, e_ref, second_ref, o_hbm, p_ref, sems):
    copies = [pltpu.make_async_copy(second_ref, o_hbm.at[pl.ds(PACKED, PACKED)], sems.at[4])]
    copies[0].start()

    def send(n, start, size):
        rows = pl.ds(start, size)
        copies.append(pltpu.make_async_copy(p_ref.at[rows], o_hbm.at[rows], sems.at[n]))
        copies[-1].start()

    weight_grad(xc_ref, xo_ref, e_ref, p_ref, lambda c: send(c, c * 3 * C, 3 * C))
    send(3, 9 * C, 5 * C)
    for copy in copies:
        copy.wait()


def finish_kernel(scale, r_ref, first_hbm, second_hbm, first_ref, second_ref, sems):
    copies = []
    for which, (ref, hbm) in enumerate(((first_ref, first_hbm), (second_ref, second_hbm))):
        for c in range(3):
            for b in range(3):
                number = 3 * c + b
                k = 3 * b + c
                t = (r_ref[pl.ds(which * PACKED + number * C, C), :].astype(f32) * scale).T
                ref[9 + k] = t[:C]
                ref[18 + k] = t[C:]
                if number % 2 == 0:
                    t = (r_ref[pl.ds(which * PACKED + (9 + number // 2) * C, C), :].astype(f32) * scale).T
                    held = t[C:]
                    ref[k] = t[:C]
                else:
                    ref[k] = held
        copy = pltpu.make_async_copy(ref, hbm, sems.at[which])
        copy.start()
        copies.append(copy)
    for copy in copies:
        copy.wait()


VMEM = pl.BlockSpec(memory_space=pltpu.VMEM)
SMEM = pl.BlockSpec(memory_space=pltpu.SMEM)
HBM = pl.BlockSpec(memory_space=pltpu.HBM)
FIELD = jax.ShapeDtypeStruct((ROWS, 128), f32)
PLANES = jax.ShapeDtypeStruct((PLANE, 128), bf16)
CENTERS = (CAP, 2, 8, 16, 768)
OUTERS = (CAP, 2, 2, 16, 768)
HALF = jax.ShapeDtypeStruct((ROWS // 2, 128), f32)
GRADS = jax.ShapeDtypeStruct((27, C, C), f32)
WEIGHTS = jax.ShapeDtypeStruct((4, 768, 256), bf16)
CUBES = jax.ShapeDtypeStruct((1, CAP, C, E * E * E), f32)
OWN = pltpu.VMEM((ROWS + 256, 128), f32)
POOL = pltpu.VMEM((2, 2 * PLANE + 32, 128), f32)
TMP = pltpu.VMEM((16, C, 128), f32)


def call(kernel, scalars, arrays, outs, scratch=(), flops=0, place=VMEM, result=VMEM):
    moved = sum(x.size * x.dtype.itemsize for x in arrays) + sum(o.size * o.dtype.itemsize for o in outs)
    return pl.pallas_call(
        kernel,
        out_shape=outs,
        in_specs=[SMEM] * len(scalars) + [place] * len(arrays),
        out_specs=[result] * len(outs),
        scratch_shapes=list(scratch),
        cost_estimate=pl.CostEstimate(flops=flops, bytes_accessed=moved, transcendentals=0),
        compiler_params=pltpu.CompilerParams(vmem_limit_bytes=24 << 20),
    )(*scalars, *arrays)


def slot_table(neighbours):
    own = neighbours - lax.axis_index("brick") * CAP
    depth = jnp.array([item[2] for item in directions], jnp.int32)[None, :]
    inside = jnp.clip(own, 0, CAP - 1)
    below = jnp.where(own >= 0, inside, jnp.clip(own + 2 * CAP, CAP, 2 * CAP - 1))
    above = jnp.clip(own, 0, 2 * CAP - 1)
    present = neighbours >= 0
    middle = jnp.where(present, inside * 256, ROWS)
    outer = jnp.where(present, jnp.where(depth < 0, below, above) * 32, 2 * PLANE)
    return jnp.where(depth == 0, middle, outer).astype(jnp.int32)


def step(features, cotangent, first_kernel, second_kernel, counts, neighbours):
    bricks = lax.axis_size("brick")
    up_pairs = [(i, (i + 1) % bricks) for i in range(bricks)]
    down_pairs = [(j, i) for i, j in up_pairs]

    def exchange(up, down):
        return lax.ppermute(up, "brick", up_pairs), lax.ppermute(down, "brick", down_pairs)

    idx = slot_table(neighbours)
    centers = jax.ShapeDtypeStruct(CENTERS, bf16)
    outers = jax.ShapeDtypeStruct(OUTERS, bf16)
    packed = jax.ShapeDtypeStruct((PACKED, 128), bf16)
    raw = pltpu.VMEM((27, C, C), f32)
    cubes = pltpu.VMEM((1, CAP, C, E * E * E), f32)
    work = 2 * ROWS * 2304 * 128
    features, cotangent, first_kernel, second_kernel = [
        pltpu.with_memory_space_constraint(v, pltpu.HBM) for v in (features, cotangent, first_kernel, second_kernel)
    ]

    def layer(formula, send, field, weights, extra, between, keep=True):
        planes = between
        xc, pc, qc = call(
            functools.partial(center_kernel, formula, len(extra)),
            [idx],
            [field, weights] + extra,
            [centers, HALF, HALF],
            [OWN],
            work // 2,
        )
        made = call(
            functools.partial(outer_kernel, formula, len(extra), send),
            [idx],
            [field, weights, *planes, xc, pc, qc] + extra,
            [FIELD, FIELD, PLANES, PLANES] + ([outers] if keep else []),
            [POOL] if keep else [pltpu.VMEM(OUTERS, bf16), POOL],
            work // 2,
        )
        p, q, up, down = made[:4]
        return xc, made[4] if keep else None, p, q, up, down

    taps = jax.ShapeDtypeStruct((27, C, C), f32)
    inputs, up, down, first_taps, raw_upstream, second_taps = call(
        pre_kernel,
        [counts],
        [features, first_kernel, cotangent, second_kernel],
        [FIELD, PLANES, PLANES, taps, CUBES, taps],
        [TMP, cubes, pltpu.SemaphoreType.DMA((4,))],
        place=HBM,
    )
    planes = exchange(up, down)
    (f1,) = call(prep1_kernel, [], [first_taps], [WEIGHTS])
    xc1, xo1, hidden, slope1, up, down = layer(lambda v, a: first_layer(a, v), 0, inputs, f1, [], planes)
    planes = exchange(up, down)
    f2, upstream = call(prep2_kernel, [counts], [second_taps, raw_upstream], [WEIGHTS, FIELD], [TMP])
    xc2, xo2, out_rows, second_err, up, down = layer(
        lambda v, a, u: second_layer(a, v, u), 1, hidden, f2, [upstream], planes
    )
    planes = exchange(up, down)
    (b2,) = call(back_kernel, [], [second_taps], [WEIGHTS])
    (second_local,) = call(w2_kernel, [], [xc2, xo2, second_err], [packed], (), work)
    _, _, hidden_grad, first_err, up, down = layer(
        lambda v, a, u, slope: second_back(v, u, slope), 1, second_err, b2, [upstream, slope1], planes, False
    )
    lo, hi = exchange(up, down)
    (partial,) = call(
        w1_kernel,
        [],
        [xc1, xo1, first_err, second_local],
        [jax.ShapeDtypeStruct((2 * PACKED, 128), bf16)],
        [pltpu.VMEM((PACKED, 128), bf16), pltpu.SemaphoreType.DMA((5,))],
        work,
        result=HBM,
    )
    (b1,) = call(back_kernel, [], [first_taps], [WEIGHTS])
    (input_grad,) = call(
        last_kernel,
        [idx],
        [first_err, lo, hi, b1, hidden_grad],
        [CUBES],
        [OWN, POOL, pltpu.VMEM(CENTERS, bf16), pltpu.VMEM(OUTERS, bf16), pltpu.VMEM((ROWS, 128), f32), TMP],
        work,
    )
    (outputs,) = call(rows_kernel, [], [out_rows], [CUBES], [TMP])
    axes = ("brick", "scene")
    scenes = lax.axis_size("scene")
    devices = bricks * scenes
    row = 4 if bricks % 4 == 0 else 1
    near, far = row * scenes, bricks // row
    near_groups = [list(range(z * near, (z + 1) * near)) for z in range(far)]
    far_groups = [[x + row * z for z in range(far)] for x in range(row)]
    share = 2 * PACKED // near

    def near_exchange(blocks):
        return lax.all_to_all(blocks, axes, 0, 0, axis_index_groups=near_groups, tiled=True)

    def far_exchange(blocks):
        return lax.all_to_all(blocks, "brick", 0, 0, axis_index_groups=far_groups, tiled=True)

    def total_of(blocks):
        return jnp.sum(blocks.astype(f32), axis=0).astype(bf16)

    def spread(block, count):
        return jnp.broadcast_to(block[None], (count,) + block.shape)

    scattered = near_exchange(partial.reshape(near, share, 128))
    mine = total_of(scattered)
    mine = total_of(far_exchange(spread(mine, far)))
    total = near_exchange(spread(mine, near))
    scale = float((devices * CAP * E * E * E) ** -0.5)
    first_grad, second_grad = call(
        functools.partial(finish_kernel, scale),
        [],
        [total.reshape(2 * PACKED, 128)],
        [GRADS, GRADS],
        [raw, raw, pltpu.SemaphoreType.DMA((2,))],
        result=HBM,
    )
    return (outputs, input_grad, first_grad, second_grad)


def solution(mesh):
    return jax.shard_map(
        step,
        mesh=mesh,
        in_specs=(
            P("scene", "brick", None, None),
            P("scene", "brick", None, None),
            P(),
            P(),
            P("brick"),
            P("brick", None),
        ),
        out_specs=(P("scene", "brick", None, None), P("scene", "brick", None, None), P(), P()),
        check_vma=False,
    )
```

```python
import functools

import jax
import jax.numpy as jnp
from jax import lax
from jax.experimental import pallas as pl
from jax.experimental.pallas import tpu as pltpu
from jax.sharding import PartitionSpec as P


E = 8
C = 64
CAP = 4
f32 = jnp.float32
bf16 = jnp.bfloat16
offsets = [(a, b, c) for a in (-1, 0, 1) for b in (-1, 0, 1) for c in (-1, 0, 1)]
directions = [item for item in offsets if item != (0, 0, 0)]
number_of = {item: n for n, item in enumerate(directions)}

ROWS = CAP * 256
PLANE = CAP * 32
PACKED = 896


def row0(s, n, l):
    return s * 256 + (n // 2) * 128 + l * 16 + (n % 2) * 8


def flip(t):
    tt = t.T
    return jnp.concatenate([tt[:C], tt[C:]], axis=1)


def lane_low(shape):
    return lax.broadcasted_iota(jnp.int32, shape, 1) < C


def to_rows(x_ref, a_ref, tmp_ref, counts_ref):
    for s in range(CAP):
        occupied = jnp.where(s < counts_ref[0], 1.0, 0.0).astype(f32)
        for n in range(4):
            t = x_ref[0, s, :, n * 128 : (n + 1) * 128] * occupied
            tmp_ref[s * 4 + n] = flip(t)
            for l in range(E):
                a_ref[pl.ds(row0(s, n, l), 8), :] = tmp_ref[s * 4 + n, pl.ds(l, 8, stride=8), :]


def from_rows(a_ref, o_ref, tmp_ref):
    for s in range(CAP):
        for n in range(4):
            for l in range(E):
                tmp_ref[s * 4 + n, pl.ds(l, 8, stride=8), :] = a_ref[pl.ds(row0(s, n, l), 8), :]
            o_ref[0, s, :, n * 128 : (n + 1) * 128] = flip(tmp_ref[s * 4 + n])


def planes_out(a_ref, up_ref, down_ref):
    for s in range(CAP):
        for nh in range(2):
            base = s * 256 + nh * 128
            to = pl.ds(s * 32 + nh * 16, 16)
            up_ref[to, :] = a_ref[pl.ds(base + 7 * 16, 16), :].astype(bf16)
            down_ref[to, :] = a_ref[pl.ds(base, 16), :].astype(bf16)


def pre_kernel(
    counts_ref, x_hbm, w1_hbm, u_hbm, w2_hbm, a_ref, up_ref, down_ref, w1_ref, u_ref, w2_ref, tmp_ref, x_ref, sems
):
    pairs = ((x_hbm, x_ref), (w1_hbm, w1_ref), (w2_hbm, w2_ref), (u_hbm, u_ref))
    copies = [pltpu.make_async_copy(src, dst, sems.at[n]) for n, (src, dst) in enumerate(pairs)]
    for copy in copies:
        copy.start()
    copies[0].wait()
    to_rows(x_ref, a_ref, tmp_ref, counts_ref)
    planes_out(a_ref, up_ref, down_ref)
    for copy in copies[1:]:
        copy.wait()


def flat_weights(w_ref, o_ref, back):
    zero = jnp.zeros((C, C), f32)

    def block(a, b, c):
        k = 9 * (a + 1) + 3 * (b + 1) + (c + 1)
        return w_ref[26 - k].T if back else w_ref[k]

    blank = jnp.zeros((256, 128), bf16)
    for bi, b in enumerate((-1, 0, 1)):
        rows = pl.ds(bi * 256, 256)
        o_ref[0, rows, 128:] = blank
        o_ref[3, rows, :128] = blank
        for ci, c in enumerate((-1, 0, 1)):
            low, mid, high = (block(a, b, c) for a in (-1, 0, 1))
            left = jnp.concatenate([mid, high, zero, low], axis=0)
            right = jnp.concatenate([low, mid, high, zero], axis=0)
            joined = jnp.concatenate([left, right], axis=1).astype(bf16)
            o_ref[ci, rows, :128] = joined
            o_ref[ci + 1, rows, 128:] = joined


def prep1_kernel(w1_ref, f1_ref):
    flat_weights(w1_ref, f1_ref, False)


def prep2_kernel(counts_ref, w2_ref, x_ref, f2_ref, u_ref, tmp_ref):
    flat_weights(w2_ref, f2_ref, False)
    to_rows(x_ref, u_ref, tmp_ref, counts_ref)


def back_kernel(w_ref, b_ref):
    flat_weights(w_ref, b_ref, True)


def build(idx_ref, source, x_ref, layers, c):
    row = lax.broadcasted_iota(jnp.int32, (8, 128), 0)
    low = lane_low((8, 128))

    def one_slot(s, carry):
        def tile(a, b, n, l):
            base = s * 256 if (a, b, c) == (0, 0, 0) else idx_ref[s, number_of[a, b, c]]
            return source(base, n, l)

        def pair(b, n, l):
            full = tile(0, b, n, l)
            after = tile(0, b, n + 1, l) if n < 3 else tile(1, b, 0, l)
            before = tile(0, b, n - 1, l) if n > 0 else tile(-1, b, 3, l)
            return full, jnp.where(low, after, before)

        for nh in range(2):
            for at, l in layers:
                parts = [[] for _ in range(6)]
                for nl in range(2):
                    n = 2 * nh + nl
                    own, left, right = pair(0, n, l), pair(-1, n, l), pair(1, n, l)
                    for h in range(2):
                        parts[h].append(pltpu.roll(jnp.where(row == 7, left[h], own[h]), 1, 0))
                        parts[2 + h].append(own[h])
                        parts[4 + h].append(pltpu.roll(jnp.where(row == 0, right[h], own[h]), 7, 0))
                for q in range(6):
                    x_ref[s, nh, at, :, q * 128 : (q + 1) * 128] = jnp.concatenate(parts[q], axis=0).astype(bf16)
        return carry

    lax.fori_loop(0, CAP, one_slot, 0)


def build_center(idx_ref, a_ref, g_ref, xc_ref):
    g_ref[pl.ds(0, ROWS), :] = a_ref[...]
    g_ref[pl.ds(ROWS, 256), :] = jnp.zeros((256, 128), f32)

    def source(base, n, l):
        return g_ref[pl.ds(pl.multiple_of(base + ((n // 2) * 128 + l * 16 + (n % 2) * 8), 8), 8), :]

    build(idx_ref, source, xc_ref, [(l, l) for l in range(E)], 0)


def build_outer(idx_ref, a_ref, lo_ref, hi_ref, pool_ref, xo_ref):
    for side, (ref, layer) in enumerate(((lo_ref, 7), (hi_ref, 0))):
        for s in range(CAP):
            for nh in range(2):
                pool_ref[side, pl.ds(s * 32 + nh * 16, 16), :] = a_ref[
                    pl.ds(s * 256 + nh * 128 + layer * 16, 16), :
                ]
        pool_ref[side, pl.ds(PLANE, PLANE), :] = ref[...].astype(f32)
        pool_ref[side, pl.ds(2 * PLANE, 32), :] = jnp.zeros((32, 128), f32)

        def source(base, n, l, side=side):
            return pool_ref[side, pl.ds(pl.multiple_of(base + ((n // 2) * 16 + (n % 2) * 8), 8), 8), :]

        build(idx_ref, source, xo_ref, [(side, 0)], -1 if side == 0 else 1)


def layers_of(xc_ref, xo_ref, first, count):
    parts = []
    if first == 0:
        parts.append(xo_ref[:, :, 0:1])
    low, high = max(first, 1), min(first + count, 9)
    if high > low:
        parts.append(xc_ref[:, :, low - 1 : high - 1])
    if first + count == 10:
        parts.append(xo_ref[:, :, 1:2])
    return parts[0] if len(parts) == 1 else jnp.concatenate(parts, axis=2)


def convolve(xc_ref, xo_ref, w_ref, firsts, epilogue):
    total = None
    count = len(firsts)
    for d in range(4):
        rows = jnp.concatenate([layers_of(xc_ref, xo_ref, l + d, 1) for l in firsts], axis=2)
        term = jnp.dot(rows.reshape(128 * count, 768), w_ref[d], preferred_element_type=f32)
        total = term if total is None else total + term
    for s in range(CAP):
        for nh in range(2):
            for i, l in enumerate(firsts):
                for h in range(2):
                    at = ((s * 2 + nh) * count + i) * 16
                    epilogue(s, nh, l + h, total[at : at + 16, h * 128 : h * 128 + 128])


def convolve_ends(xc_ref, xo_ref, w_ref, epilogue):
    total = None
    for c in range(3):
        rows = jnp.concatenate([layers_of(xc_ref, xo_ref, l + c, 1) for l in (0, 7)], axis=2)
        term = jnp.dot(rows.reshape(256, 768), w_ref[c, :, :128], preferred_element_type=f32)
        total = term if total is None else total + term
    for s in range(CAP):
        for nh in range(2):
            for i, l in enumerate((0, 7)):
                at = ((s * 2 + nh) * 2 + i) * 16
                epilogue(s, nh, l, total[at : at + 16])


CENTER = (1, 3, 5)
ALL = (0, 2, 4, 6)


def full_rows(s, nh, l):
    return pl.ds(s * 256 + nh * 128 + l * 16, 16)


def center_rows(s, nh, l):
    return pl.ds((s * 2 + nh) * 96 + (l - 1) * 16, 16)


def take_center(part_ref, full_ref):
    for s in range(CAP):
        for nh in range(2):
            full_ref[pl.ds(s * 256 + nh * 128 + 16, 96), :] = part_ref[pl.ds((s * 2 + nh) * 96, 96), :]


def logistic(v):
    return 1.0 / (1.0 + jnp.exp(-v))


def first_layer(a, v):
    q = logistic(v)
    return a + v * q, q * (1.0 + v * (1.0 - q))


def second_layer(a, v, u):
    q = logistic(v)
    return a + v * q, u * (q * (1.0 + v * (1.0 - q)))


def second_back(v, u, slope):
    grad = u + v
    return grad, grad * slope


def center_kernel(formula, count, idx_ref, a_ref, w_ref, *refs):
    extra, (xc_ref, p_ref, q_ref, g_ref) = refs[:count], refs[count:]
    build_center(idx_ref, a_ref, g_ref, xc_ref)

    def epilogue(s, nh, l, v):
        full, part = full_rows(s, nh, l), center_rows(s, nh, l)
        p_ref[part, :], q_ref[part, :] = formula(v, a_ref[full, :], *[r[full, :] for r in extra])

    convolve(xc_ref, None, w_ref, CENTER, epilogue)


def outer_kernel(formula, count, send, idx_ref, a_ref, w_ref, lo_ref, hi_ref, xc_ref, pc_ref, qc_ref, *refs):
    extra, (p_ref, q_ref, up_ref, down_ref, xo_ref, pool_ref) = refs[:count], refs[count:]
    build_outer(idx_ref, a_ref, lo_ref, hi_ref, pool_ref, xo_ref)

    def epilogue(s, nh, l, v):
        full = full_rows(s, nh, l)
        p_ref[full, :], q_ref[full, :] = formula(v, a_ref[full, :], *[r[full, :] for r in extra])

    convolve_ends(xc_ref, xo_ref, w_ref, epilogue)
    planes_out((p_ref, q_ref)[send], up_ref, down_ref)
    take_center(pc_ref, p_ref)
    take_center(qc_ref, q_ref)


def last_kernel(idx_ref, a_ref, lo_ref, hi_ref, w_ref, hg_ref, o_ref, g_ref, pool_ref, xc_ref, xo_ref, r_ref, tmp_ref):
    build_center(idx_ref, a_ref, g_ref, xc_ref)
    build_outer(idx_ref, a_ref, lo_ref, hi_ref, pool_ref, xo_ref)

    def epilogue(s, nh, l, v):
        full = full_rows(s, nh, l)
        r_ref[full, :] = hg_ref[full, :] + v

    convolve(xc_ref, xo_ref, w_ref, ALL, epilogue)
    from_rows(r_ref, o_ref, tmp_ref)


def rows_kernel(r_ref, o_ref, tmp_ref):
    from_rows(r_ref, o_ref, tmp_ref)


def weight_grad(xc_ref, xo_ref, e_ref, p_ref, ready=None):
    low = lane_low((C, 128))
    errors = e_ref[...].T.astype(bf16)
    held = None
    for c in range(3):
        rows = layers_of(xc_ref, xo_ref, c, E).reshape(ROWS, 768)
        m = jnp.dot(errors, rows, preferred_element_type=f32)
        for b in range(3):
            number = 3 * c + b
            z0, z1 = m[:C, b * 256 : b * 256 + 128], m[C:, b * 256 : b * 256 + 128]
            y0, y1 = m[:C, b * 256 + 128 : (b + 1) * 256], m[C:, b * 256 + 128 : (b + 1) * 256]
            p_ref[pl.ds(number * C, C), :] = (z0 + pltpu.roll(jnp.where(low, y1, z1), C, 1)).astype(p_ref.dtype)
            if number % 2 == 0:
                held = z1 + pltpu.roll(y0, C, 1)
                if number == 8:
                    p_ref[pl.ds((9 + number // 2) * C, C), :] = jnp.where(low, held, 0.0).astype(p_ref.dtype)
            else:
                odd = pltpu.roll(z1, C, 1) + y0
                p_ref[pl.ds((9 + number // 2) * C, C), :] = jnp.where(low, held, odd).astype(p_ref.dtype)
        if ready is not None:
            ready(c)


def w2_kernel(xc_ref, xo_ref, e_ref, p_ref):
    weight_grad(xc_ref, xo_ref, e_ref, p_ref)


def w1_kernel(xc_ref, xo_ref, e_ref, second_ref, o_hbm, p_ref, sems):
    copies = [pltpu.make_async_copy(second_ref, o_hbm.at[pl.ds(PACKED, PACKED)], sems.at[4])]
    copies[0].start()

    def send(n, start, size):
        rows = pl.ds(start, size)
        copies.append(pltpu.make_async_copy(p_ref.at[rows], o_hbm.at[rows], sems.at[n]))
        copies[-1].start()

    weight_grad(xc_ref, xo_ref, e_ref, p_ref, lambda c: send(c, c * 3 * C, 3 * C))
    send(3, 9 * C, 5 * C)
    for copy in copies:
        copy.wait()


def finish_kernel(scale, r_ref, first_hbm, second_hbm, first_ref, second_ref, sems):
    copies = []
    for which, (ref, hbm) in enumerate(((first_ref, first_hbm), (second_ref, second_hbm))):
        for c in range(3):
            for b in range(3):
                number = 3 * c + b
                k = 3 * b + c
                t = (r_ref[pl.ds(which * PACKED + number * C, C), :].astype(f32) * scale).T
                ref[9 + k] = t[:C]
                ref[18 + k] = t[C:]
                if number % 2 == 0:
                    t = (r_ref[pl.ds(which * PACKED + (9 + number // 2) * C, C), :].astype(f32) * scale).T
                    held = t[C:]
                    ref[k] = t[:C]
                else:
                    ref[k] = held
        copy = pltpu.make_async_copy(ref, hbm, sems.at[which])
        copy.start()
        copies.append(copy)
    for copy in copies:
        copy.wait()


VMEM = pl.BlockSpec(memory_space=pltpu.VMEM)
SMEM = pl.BlockSpec(memory_space=pltpu.SMEM)
HBM = pl.BlockSpec(memory_space=pltpu.HBM)
FIELD = jax.ShapeDtypeStruct((ROWS, 128), f32)
PLANES = jax.ShapeDtypeStruct((PLANE, 128), bf16)
CENTERS = (CAP, 2, 8, 16, 768)
OUTERS = (CAP, 2, 2, 16, 768)
MIDDLE = jax.ShapeDtypeStruct((ROWS * 3 // 4, 128), f32)
GRADS = jax.ShapeDtypeStruct((27, C, C), f32)
WEIGHTS = jax.ShapeDtypeStruct((4, 768, 256), bf16)
CUBES = jax.ShapeDtypeStruct((1, CAP, C, E * E * E), f32)
OWN = pltpu.VMEM((ROWS + 256, 128), f32)
POOL = pltpu.VMEM((2, 2 * PLANE + 32, 128), f32)
TMP = pltpu.VMEM((16, C, 128), f32)


def call(kernel, scalars, arrays, outs, scratch=(), flops=0, place=VMEM, result=VMEM):
    moved = sum(x.size * x.dtype.itemsize for x in arrays) + sum(o.size * o.dtype.itemsize for o in outs)
    return pl.pallas_call(
        kernel,
        out_shape=outs,
        in_specs=[SMEM] * len(scalars) + [place] * len(arrays),
        out_specs=[result] * len(outs),
        scratch_shapes=list(scratch),
        cost_estimate=pl.CostEstimate(flops=flops, bytes_accessed=moved, transcendentals=0),
        compiler_params=pltpu.CompilerParams(vmem_limit_bytes=24 << 20),
    )(*scalars, *arrays)


def slot_table(neighbours):
    own = neighbours - lax.axis_index("brick") * CAP
    depth = jnp.array([item[2] for item in directions], jnp.int32)[None, :]
    inside = jnp.clip(own, 0, CAP - 1)
    below = jnp.where(own >= 0, inside, jnp.clip(own + 2 * CAP, CAP, 2 * CAP - 1))
    above = jnp.clip(own, 0, 2 * CAP - 1)
    present = neighbours >= 0
    middle = jnp.where(present, inside * 256, ROWS)
    outer = jnp.where(present, jnp.where(depth < 0, below, above) * 32, 2 * PLANE)
    return jnp.where(depth == 0, middle, outer).astype(jnp.int32)


def step(features, cotangent, first_kernel, second_kernel, counts, neighbours):
    bricks = lax.axis_size("brick")
    up_pairs = [(i, (i + 1) % bricks) for i in range(bricks)]
    down_pairs = [(j, i) for i, j in up_pairs]

    def exchange(up, down):
        return lax.ppermute(up, "brick", up_pairs), lax.ppermute(down, "brick", down_pairs)

    idx = slot_table(neighbours)
    centers = jax.ShapeDtypeStruct(CENTERS, bf16)
    outers = jax.ShapeDtypeStruct(OUTERS, bf16)
    packed = jax.ShapeDtypeStruct((PACKED, 128), bf16)
    raw = pltpu.VMEM((27, C, C), f32)
    cubes = pltpu.VMEM((1, CAP, C, E * E * E), f32)
    work = 2 * ROWS * 2304 * 128
    features, cotangent, first_kernel, second_kernel = [
        pltpu.with_memory_space_constraint(v, pltpu.HBM) for v in (features, cotangent, first_kernel, second_kernel)
    ]

    def layer(formula, send, field, weights, extra, between, keep=True):
        planes = between
        xc, pc, qc = call(
            functools.partial(center_kernel, formula, len(extra)),
            [idx],
            [field, weights] + extra,
            [centers, MIDDLE, MIDDLE],
            [OWN],
            work // 2,
        )
        made = call(
            functools.partial(outer_kernel, formula, len(extra), send),
            [idx],
            [field, weights, *planes, xc, pc, qc] + extra,
            [FIELD, FIELD, PLANES, PLANES] + ([outers] if keep else []),
            [POOL] if keep else [pltpu.VMEM(OUTERS, bf16), POOL],
            work // 2,
        )
        p, q, up, down = made[:4]
        return xc, made[4] if keep else None, p, q, up, down

    taps = jax.ShapeDtypeStruct((27, C, C), f32)
    inputs, up, down, first_taps, raw_upstream, second_taps = call(
        pre_kernel,
        [counts],
        [features, first_kernel, cotangent, second_kernel],
        [FIELD, PLANES, PLANES, taps, CUBES, taps],
        [TMP, cubes, pltpu.SemaphoreType.DMA((4,))],
        place=HBM,
    )
    planes = exchange(up, down)
    (f1,) = call(prep1_kernel, [], [first_taps], [WEIGHTS])
    xc1, xo1, hidden, slope1, up, down = layer(lambda v, a: first_layer(a, v), 0, inputs, f1, [], planes)
    planes = exchange(up, down)
    f2, upstream = call(prep2_kernel, [counts], [second_taps, raw_upstream], [WEIGHTS, FIELD], [TMP])
    xc2, xo2, out_rows, second_err, up, down = layer(
        lambda v, a, u: second_layer(a, v, u), 1, hidden, f2, [upstream], planes
    )
    planes = exchange(up, down)
    (b2,) = call(back_kernel, [], [second_taps], [WEIGHTS])
    (second_local,) = call(w2_kernel, [], [xc2, xo2, second_err], [packed], (), work)
    _, _, hidden_grad, first_err, up, down = layer(
        lambda v, a, u, slope: second_back(v, u, slope), 1, second_err, b2, [upstream, slope1], planes, False
    )
    lo, hi = exchange(up, down)
    (partial,) = call(
        w1_kernel,
        [],
        [xc1, xo1, first_err, second_local],
        [jax.ShapeDtypeStruct((2 * PACKED, 128), bf16)],
        [pltpu.VMEM((PACKED, 128), bf16), pltpu.SemaphoreType.DMA((5,))],
        work,
        result=HBM,
    )
    (b1,) = call(back_kernel, [], [first_taps], [WEIGHTS])
    (input_grad,) = call(
        last_kernel,
        [idx],
        [first_err, lo, hi, b1, hidden_grad],
        [CUBES],
        [OWN, POOL, pltpu.VMEM(CENTERS, bf16), pltpu.VMEM(OUTERS, bf16), pltpu.VMEM((ROWS, 128), f32), TMP],
        work,
    )
    (outputs,) = call(rows_kernel, [], [out_rows], [CUBES], [TMP])
    axes = ("brick", "scene")
    scenes = lax.axis_size("scene")
    devices = bricks * scenes
    row = 4 if bricks % 4 == 0 else 1
    near, far = row * scenes, bricks // row
    near_groups = [list(range(z * near, (z + 1) * near)) for z in range(far)]
    far_groups = [[x + row * z for z in range(far)] for x in range(row)]
    share = 2 * PACKED // near

    def near_exchange(blocks):
        return lax.all_to_all(blocks, axes, 0, 0, axis_index_groups=near_groups, tiled=True)

    def far_exchange(blocks):
        return lax.all_to_all(blocks, "brick", 0, 0, axis_index_groups=far_groups, tiled=True)

    def total_of(blocks):
        return jnp.sum(blocks.astype(f32), axis=0).astype(bf16)

    def spread(block, count):
        return jnp.broadcast_to(block[None], (count,) + block.shape)

    scattered = near_exchange(partial.reshape(near, share, 128))
    mine = total_of(scattered)
    mine = total_of(far_exchange(spread(mine, far)))
    total = near_exchange(spread(mine, near))
    scale = float((devices * CAP * E * E * E) ** -0.5)
    first_grad, second_grad = call(
        functools.partial(finish_kernel, scale),
        [],
        [total.reshape(2 * PACKED, 128)],
        [GRADS, GRADS],
        [raw, raw, pltpu.SemaphoreType.DMA((2,))],
        result=HBM,
    )
    return (outputs, input_grad, first_grad, second_grad)


def solution(mesh):
    return jax.shard_map(
        step,
        mesh=mesh,
        in_specs=(
            P("scene", "brick", None, None),
            P("scene", "brick", None, None),
            P(),
            P(),
            P("brick"),
            P("brick", None),
        ),
        out_specs=(P("scene", "brick", None, None), P("scene", "brick", None, None), P(), P()),
        check_vma=False,
    )
```

```python
import functools

import jax
import jax.numpy as jnp
from jax import lax
from jax.experimental import pallas as pl
from jax.experimental.pallas import tpu as pltpu
from jax.sharding import PartitionSpec as P


E = 8
C = 64
CAP = 4
f32 = jnp.float32
bf16 = jnp.bfloat16
offsets = [(a, b, c) for a in (-1, 0, 1) for b in (-1, 0, 1) for c in (-1, 0, 1)]
directions = [item for item in offsets if item != (0, 0, 0)]
number_of = {item: n for n, item in enumerate(directions)}

ROWS = CAP * 256
PLANE = CAP * 32
PACKED = 896


def row0(s, n, l):
    return s * 256 + (n // 2) * 128 + l * 16 + (n % 2) * 8


def flip(t):
    tt = t.T
    return jnp.concatenate([tt[:C], tt[C:]], axis=1)


def lane_low(shape):
    return lax.broadcasted_iota(jnp.int32, shape, 1) < C


def to_rows(x_ref, a_ref, tmp_ref, counts_ref):
    for s in range(CAP):
        occupied = jnp.where(s < counts_ref[0], 1.0, 0.0).astype(f32)
        for n in range(4):
            t = x_ref[0, s, :, n * 128 : (n + 1) * 128] * occupied
            tmp_ref[s * 4 + n] = flip(t)
            for l in range(E):
                a_ref[pl.ds(row0(s, n, l), 8), :] = tmp_ref[s * 4 + n, pl.ds(l, 8, stride=8), :]


def from_rows(a_ref, o_ref, tmp_ref):
    for s in range(CAP):
        for n in range(4):
            for l in range(E):
                tmp_ref[s * 4 + n, pl.ds(l, 8, stride=8), :] = a_ref[pl.ds(row0(s, n, l), 8), :]
            o_ref[0, s, :, n * 128 : (n + 1) * 128] = flip(tmp_ref[s * 4 + n])


def planes_out(a_ref, up_ref, down_ref):
    for s in range(CAP):
        for nh in range(2):
            base = s * 256 + nh * 128
            to = pl.ds(s * 32 + nh * 16, 16)
            up_ref[to, :] = a_ref[pl.ds(base + 7 * 16, 16), :].astype(bf16)
            down_ref[to, :] = a_ref[pl.ds(base, 16), :].astype(bf16)


def pre_kernel(
    counts_ref, x_hbm, w1_hbm, u_hbm, w2_hbm, a_ref, up_ref, down_ref, w1_ref, u_ref, w2_ref, tmp_ref, x_ref, sems
):
    pairs = ((x_hbm, x_ref), (w1_hbm, w1_ref), (w2_hbm, w2_ref), (u_hbm, u_ref))
    copies = [pltpu.make_async_copy(src, dst, sems.at[n]) for n, (src, dst) in enumerate(pairs)]
    for copy in copies:
        copy.start()
    copies[0].wait()
    to_rows(x_ref, a_ref, tmp_ref, counts_ref)
    planes_out(a_ref, up_ref, down_ref)
    for copy in copies[1:]:
        copy.wait()


def flat_weights(w_ref, o_ref, back):
    zero = jnp.zeros((C, C), f32)

    def block(a, b, c):
        k = 9 * (a + 1) + 3 * (b + 1) + (c + 1)
        return w_ref[26 - k].T if back else w_ref[k]

    blank = jnp.zeros((256, 128), bf16)
    for bi, b in enumerate((-1, 0, 1)):
        rows = pl.ds(bi * 256, 256)
        o_ref[0, rows, 128:] = blank
        o_ref[3, rows, :128] = blank
        for ci, c in enumerate((-1, 0, 1)):
            low, mid, high = (block(a, b, c) for a in (-1, 0, 1))
            left = jnp.concatenate([mid, high, zero, low], axis=0)
            right = jnp.concatenate([low, mid, high, zero], axis=0)
            joined = jnp.concatenate([left, right], axis=1).astype(bf16)
            o_ref[ci, rows, :128] = joined
            o_ref[ci + 1, rows, 128:] = joined


def prep1_kernel(w1_ref, f1_ref):
    flat_weights(w1_ref, f1_ref, False)


def prep2_kernel(counts_ref, w2_ref, x_ref, f2_ref, u_ref, tmp_ref):
    flat_weights(w2_ref, f2_ref, False)
    to_rows(x_ref, u_ref, tmp_ref, counts_ref)


def back_kernel(w_ref, b_ref):
    flat_weights(w_ref, b_ref, True)


def build(idx_ref, source, x_ref, layers, c):
    row = lax.broadcasted_iota(jnp.int32, (8, 128), 0)
    low = lane_low((8, 128))

    def one_slot(s, carry):
        def tile(a, b, n, l):
            base = s * 256 if (a, b, c) == (0, 0, 0) else idx_ref[s, number_of[a, b, c]]
            return source(base, n, l)

        def pair(b, n, l):
            full = tile(0, b, n, l)
            after = tile(0, b, n + 1, l) if n < 3 else tile(1, b, 0, l)
            before = tile(0, b, n - 1, l) if n > 0 else tile(-1, b, 3, l)
            return full, jnp.where(low, after, before)

        for nh in range(2):
            for at, l in layers:
                parts = [[] for _ in range(6)]
                for nl in range(2):
                    n = 2 * nh + nl
                    own, left, right = pair(0, n, l), pair(-1, n, l), pair(1, n, l)
                    for h in range(2):
                        parts[h].append(pltpu.roll(jnp.where(row == 7, left[h], own[h]), 1, 0))
                        parts[2 + h].append(own[h])
                        parts[4 + h].append(pltpu.roll(jnp.where(row == 0, right[h], own[h]), 7, 0))
                for q in range(6):
                    x_ref[s, nh, at, :, q * 128 : (q + 1) * 128] = jnp.concatenate(parts[q], axis=0).astype(bf16)
        return carry

    lax.fori_loop(0, CAP, one_slot, 0)


def build_center(idx_ref, a_ref, g_ref, xc_ref):
    g_ref[pl.ds(0, ROWS), :] = a_ref[...]
    g_ref[pl.ds(ROWS, 256), :] = jnp.zeros((256, 128), f32)

    def source(base, n, l):
        return g_ref[pl.ds(pl.multiple_of(base + ((n // 2) * 128 + l * 16 + (n % 2) * 8), 8), 8), :]

    build(idx_ref, source, xc_ref, [(l, l) for l in range(E)], 0)


def build_outer(idx_ref, a_ref, lo_ref, hi_ref, pool_ref, xo_ref):
    for side, (ref, layer) in enumerate(((lo_ref, 7), (hi_ref, 0))):
        for s in range(CAP):
            for nh in range(2):
                pool_ref[side, pl.ds(s * 32 + nh * 16, 16), :] = a_ref[
                    pl.ds(s * 256 + nh * 128 + layer * 16, 16), :
                ]
        pool_ref[side, pl.ds(PLANE, PLANE), :] = ref[...].astype(f32)
        pool_ref[side, pl.ds(2 * PLANE, 32), :] = jnp.zeros((32, 128), f32)

        def source(base, n, l, side=side):
            return pool_ref[side, pl.ds(pl.multiple_of(base + ((n // 2) * 16 + (n % 2) * 8), 8), 8), :]

        build(idx_ref, source, xo_ref, [(side, 0)], -1 if side == 0 else 1)


def layers_of(xc_ref, xo_ref, first, count):
    parts = []
    if first == 0:
        parts.append(xo_ref[:, :, 0:1])
    low, high = max(first, 1), min(first + count, 9)
    if high > low:
        parts.append(xc_ref[:, :, low - 1 : high - 1])
    if first + count == 10:
        parts.append(xo_ref[:, :, 1:2])
    return parts[0] if len(parts) == 1 else jnp.concatenate(parts, axis=2)


def convolve(xc_ref, xo_ref, w_ref, firsts, epilogue):
    total = None
    count = len(firsts)
    for d in range(4):
        rows = jnp.concatenate([layers_of(xc_ref, xo_ref, l + d, 1) for l in firsts], axis=2)
        term = jnp.dot(rows.reshape(128 * count, 768), w_ref[d], preferred_element_type=f32)
        total = term if total is None else total + term
    for s in range(CAP):
        for nh in range(2):
            for i, l in enumerate(firsts):
                for h in range(2):
                    at = ((s * 2 + nh) * count + i) * 16
                    epilogue(s, nh, l + h, total[at : at + 16, h * 128 : h * 128 + 128])


def convolve_ends(xc_ref, xo_ref, w_ref, epilogue):
    total = None
    for c in range(3):
        rows = jnp.concatenate([layers_of(xc_ref, xo_ref, l + c, 1) for l in (0, 7)], axis=2)
        term = jnp.dot(rows.reshape(256, 768), w_ref[c, :, :128], preferred_element_type=f32)
        total = term if total is None else total + term
    for s in range(CAP):
        for nh in range(2):
            for i, l in enumerate((0, 7)):
                at = ((s * 2 + nh) * 2 + i) * 16
                epilogue(s, nh, l, total[at : at + 16])


CENTER = (1, 3, 5)
ALL = (0, 2, 4, 6)


def full_rows(s, nh, l):
    return pl.ds(s * 256 + nh * 128 + l * 16, 16)


def center_rows(s, nh, l):
    return pl.ds((s * 2 + nh) * 96 + (l - 1) * 16, 16)


def take_center(part_ref, full_ref):
    for s in range(CAP):
        for nh in range(2):
            full_ref[pl.ds(s * 256 + nh * 128 + 16, 96), :] = part_ref[pl.ds((s * 2 + nh) * 96, 96), :]


def logistic(v):
    return 1.0 / (1.0 + jnp.exp(-v))


def first_layer(a, v):
    q = logistic(v)
    return a + v * q, q * (1.0 + v * (1.0 - q))


def second_layer(a, v, u):
    q = logistic(v)
    return a + v * q, u * (q * (1.0 + v * (1.0 - q)))


def second_back(v, u, slope):
    grad = u + v
    return grad, grad * slope


def center_kernel(formula, count, idx_ref, a_ref, w_ref, *refs):
    extra, (xc_ref, p_ref, q_ref, g_ref) = refs[:count], refs[count:]
    build_center(idx_ref, a_ref, g_ref, xc_ref)

    def epilogue(s, nh, l, v):
        full, part = full_rows(s, nh, l), center_rows(s, nh, l)
        p_ref[part, :], q_ref[part, :] = formula(v, a_ref[full, :], *[r[full, :] for r in extra])

    convolve(xc_ref, None, w_ref, CENTER, epilogue)


def outer_kernel(formula, count, send, idx_ref, a_ref, w_ref, lo_ref, hi_ref, xc_ref, pc_ref, qc_ref, *refs):
    extra, (p_ref, q_ref, up_ref, down_ref, xo_ref, pool_ref) = refs[:count], refs[count:]
    build_outer(idx_ref, a_ref, lo_ref, hi_ref, pool_ref, xo_ref)

    def epilogue(s, nh, l, v):
        full = full_rows(s, nh, l)
        p_ref[full, :], q_ref[full, :] = formula(v, a_ref[full, :], *[r[full, :] for r in extra])

    convolve_ends(xc_ref, xo_ref, w_ref, epilogue)
    planes_out((p_ref, q_ref)[send], up_ref, down_ref)
    take_center(pc_ref, p_ref)
    take_center(qc_ref, q_ref)


def last_kernel(idx_ref, a_ref, lo_ref, hi_ref, w_ref, hg_ref, o_ref, g_ref, pool_ref, xc_ref, xo_ref, r_ref, tmp_ref):
    build_center(idx_ref, a_ref, g_ref, xc_ref)
    build_outer(idx_ref, a_ref, lo_ref, hi_ref, pool_ref, xo_ref)

    def epilogue(s, nh, l, v):
        full = full_rows(s, nh, l)
        r_ref[full, :] = hg_ref[full, :] + v

    convolve(xc_ref, xo_ref, w_ref, ALL, epilogue)
    from_rows(r_ref, o_ref, tmp_ref)


def rows_kernel(r_ref, o_ref, tmp_ref):
    from_rows(r_ref, o_ref, tmp_ref)


def weight_grad(xc_ref, xo_ref, e_ref, p_ref):
    low = lane_low((C, 128))
    errors = e_ref[...].T.astype(bf16)
    held = None
    for c in range(3):
        rows = layers_of(xc_ref, xo_ref, c, E).reshape(ROWS, 768)
        m = jnp.dot(errors, rows, preferred_element_type=f32)
        for b in range(3):
            number = 3 * c + b
            z0, z1 = m[:C, b * 256 : b * 256 + 128], m[C:, b * 256 : b * 256 + 128]
            y0, y1 = m[:C, b * 256 + 128 : (b + 1) * 256], m[C:, b * 256 + 128 : (b + 1) * 256]
            p_ref[pl.ds(number * C, C), :] = (z0 + pltpu.roll(jnp.where(low, y1, z1), C, 1)).astype(p_ref.dtype)
            if number % 2 == 0:
                held = z1 + pltpu.roll(y0, C, 1)
                if number == 8:
                    p_ref[pl.ds((9 + number // 2) * C, C), :] = jnp.where(low, held, 0.0).astype(p_ref.dtype)
            else:
                odd = pltpu.roll(z1, C, 1) + y0
                p_ref[pl.ds((9 + number // 2) * C, C), :] = jnp.where(low, held, odd).astype(p_ref.dtype)


def terms_kernel(xc_ref, xo_ref, e_ref, p_ref):
    weight_grad(xc_ref, xo_ref, e_ref, p_ref)


def finish_kernel(scale, r1_ref, r2_ref, first_hbm, second_hbm, first_ref, second_ref, sems):
    copies = []
    for which, (r_ref, ref, hbm) in enumerate(((r1_ref, first_ref, first_hbm), (r2_ref, second_ref, second_hbm))):
        for c in range(3):
            for b in range(3):
                number = 3 * c + b
                k = 3 * b + c
                t = (r_ref[pl.ds(number * C, C), :].astype(f32) * scale).T
                ref[9 + k] = t[:C]
                ref[18 + k] = t[C:]
                if number % 2 == 0:
                    t = (r_ref[pl.ds((9 + number // 2) * C, C), :].astype(f32) * scale).T
                    held = t[C:]
                    ref[k] = t[:C]
                else:
                    ref[k] = held
        copy = pltpu.make_async_copy(ref, hbm, sems.at[which])
        copy.start()
        copies.append(copy)
    for copy in copies:
        copy.wait()


VMEM = pl.BlockSpec(memory_space=pltpu.VMEM)
SMEM = pl.BlockSpec(memory_space=pltpu.SMEM)
HBM = pl.BlockSpec(memory_space=pltpu.HBM)
FIELD = jax.ShapeDtypeStruct((ROWS, 128), f32)
PLANES = jax.ShapeDtypeStruct((PLANE, 128), bf16)
CENTERS = (CAP, 2, 8, 16, 768)
OUTERS = (CAP, 2, 2, 16, 768)
MIDDLE = jax.ShapeDtypeStruct((ROWS * 3 // 4, 128), f32)
GRADS = jax.ShapeDtypeStruct((27, C, C), f32)
WEIGHTS = jax.ShapeDtypeStruct((4, 768, 256), bf16)
CUBES = jax.ShapeDtypeStruct((1, CAP, C, E * E * E), f32)
OWN = pltpu.VMEM((ROWS + 256, 128), f32)
POOL = pltpu.VMEM((2, 2 * PLANE + 32, 128), f32)
TMP = pltpu.VMEM((16, C, 128), f32)


def call(kernel, scalars, arrays, outs, scratch=(), flops=0, place=VMEM, result=VMEM):
    moved = sum(x.size * x.dtype.itemsize for x in arrays) + sum(o.size * o.dtype.itemsize for o in outs)
    return pl.pallas_call(
        kernel,
        out_shape=outs,
        in_specs=[SMEM] * len(scalars) + [place] * len(arrays),
        out_specs=[result] * len(outs),
        scratch_shapes=list(scratch),
        cost_estimate=pl.CostEstimate(flops=flops, bytes_accessed=moved, transcendentals=0),
        compiler_params=pltpu.CompilerParams(vmem_limit_bytes=24 << 20),
    )(*scalars, *arrays)


def slot_table(neighbours):
    own = neighbours - lax.axis_index("brick") * CAP
    depth = jnp.array([item[2] for item in directions], jnp.int32)[None, :]
    inside = jnp.clip(own, 0, CAP - 1)
    below = jnp.where(own >= 0, inside, jnp.clip(own + 2 * CAP, CAP, 2 * CAP - 1))
    above = jnp.clip(own, 0, 2 * CAP - 1)
    present = neighbours >= 0
    middle = jnp.where(present, inside * 256, ROWS)
    outer = jnp.where(present, jnp.where(depth < 0, below, above) * 32, 2 * PLANE)
    return jnp.where(depth == 0, middle, outer).astype(jnp.int32)


def step(features, cotangent, first_kernel, second_kernel, counts, neighbours):
    bricks = lax.axis_size("brick")
    up_pairs = [(i, (i + 1) % bricks) for i in range(bricks)]
    down_pairs = [(j, i) for i, j in up_pairs]

    def exchange(up, down):
        return lax.ppermute(up, "brick", up_pairs), lax.ppermute(down, "brick", down_pairs)

    idx = slot_table(neighbours)
    centers = jax.ShapeDtypeStruct(CENTERS, bf16)
    outers = jax.ShapeDtypeStruct(OUTERS, bf16)
    packed = jax.ShapeDtypeStruct((PACKED, 128), bf16)
    raw = pltpu.VMEM((27, C, C), f32)
    cubes = pltpu.VMEM((1, CAP, C, E * E * E), f32)
    work = 2 * ROWS * 2304 * 128
    features, cotangent, first_kernel, second_kernel = [
        pltpu.with_memory_space_constraint(v, pltpu.HBM) for v in (features, cotangent, first_kernel, second_kernel)
    ]

    def layer(formula, send, field, weights, extra, between, keep=True):
        planes = between
        xc, pc, qc = call(
            functools.partial(center_kernel, formula, len(extra)),
            [idx],
            [field, weights] + extra,
            [centers, MIDDLE, MIDDLE],
            [OWN],
            work // 2,
        )
        made = call(
            functools.partial(outer_kernel, formula, len(extra), send),
            [idx],
            [field, weights, *planes, xc, pc, qc] + extra,
            [FIELD, FIELD, PLANES, PLANES] + ([outers] if keep else []),
            [POOL] if keep else [pltpu.VMEM(OUTERS, bf16), POOL],
            work // 2,
        )
        p, q, up, down = made[:4]
        return xc, made[4] if keep else None, p, q, up, down

    taps = jax.ShapeDtypeStruct((27, C, C), f32)
    inputs, up, down, first_taps, raw_upstream, second_taps = call(
        pre_kernel,
        [counts],
        [features, first_kernel, cotangent, second_kernel],
        [FIELD, PLANES, PLANES, taps, CUBES, taps],
        [TMP, cubes, pltpu.SemaphoreType.DMA((4,))],
        place=HBM,
    )
    planes = exchange(up, down)
    (f1,) = call(prep1_kernel, [], [first_taps], [WEIGHTS])
    xc1, xo1, hidden, slope1, up, down = layer(lambda v, a: first_layer(a, v), 0, inputs, f1, [], planes)
    planes = exchange(up, down)
    f2, upstream = call(prep2_kernel, [counts], [second_taps, raw_upstream], [WEIGHTS, FIELD], [TMP])
    xc2, xo2, out_rows, second_err, up, down = layer(
        lambda v, a, u: second_layer(a, v, u), 1, hidden, f2, [upstream], planes
    )
    planes = exchange(up, down)
    (b2,) = call(back_kernel, [], [second_taps], [WEIGHTS])
    (second_local,) = call(terms_kernel, [], [xc2, xo2, second_err], [packed], (), work)
    _, _, hidden_grad, first_err, up, down = layer(
        lambda v, a, u, slope: second_back(v, u, slope), 1, second_err, b2, [upstream, slope1], planes, False
    )
    lo, hi = exchange(up, down)
    (first_local,) = call(terms_kernel, [], [xc1, xo1, first_err], [packed], (), work)
    (b1,) = call(back_kernel, [], [first_taps], [WEIGHTS])
    (input_grad,) = call(
        last_kernel,
        [idx],
        [first_err, lo, hi, b1, hidden_grad],
        [CUBES],
        [OWN, POOL, pltpu.VMEM(CENTERS, bf16), pltpu.VMEM(OUTERS, bf16), pltpu.VMEM((ROWS, 128), f32), TMP],
        work,
    )
    (outputs,) = call(rows_kernel, [], [out_rows], [CUBES], [TMP])
    axes = ("brick", "scene")
    scenes = lax.axis_size("scene")
    devices = bricks * scenes
    row = 4 if bricks % 4 == 0 else 1
    near, far = row * (scenes // 2), bricks // row
    near_groups = [
        [(row * z + x) * scenes + 2 * y + core for x in range(row) for y in range(scenes // 2)]
        for z in range(far)
        for core in range(2)
    ]
    far_groups = [[x + row * z for z in range(far)] for x in range(row)]
    share = PACKED // near
    pairs = [[i, i + 1] for i in range(0, scenes, 2)]
    swap = [(i, i ^ 1) for i in range(scenes)]
    even = lax.axis_index("scene") % 2 == 0

    def core_exchange(blocks):
        return lax.all_to_all(blocks, "scene", 0, 0, axis_index_groups=pairs, tiled=True)

    def near_exchange(blocks):
        return lax.all_to_all(blocks, axes, 0, 0, axis_index_groups=near_groups, tiled=True)

    def far_exchange(blocks):
        return lax.all_to_all(blocks, "brick", 0, 0, axis_index_groups=far_groups, tiled=True)

    def total_of(blocks):
        return jnp.sum(blocks.astype(f32), axis=0).astype(bf16)

    def spread(block, count):
        return jnp.broadcast_to(block[None], (count,) + block.shape)

    partial = total_of(core_exchange(jnp.stack([first_local, second_local])))
    scattered = near_exchange(partial.reshape(near, share, 128))
    mine = total_of(scattered)
    mine = total_of(far_exchange(spread(mine, far)))
    gathered = near_exchange(spread(mine, near))
    half = gathered.reshape(PACKED, 128)
    other = lax.ppermute(half, "scene", swap)
    first_total, second_total = jnp.where(even, half, other), jnp.where(even, other, half)
    scale = float((devices * CAP * E * E * E) ** -0.5)
    first_grad, second_grad = call(
        functools.partial(finish_kernel, scale),
        [],
        [first_total, second_total],
        [GRADS, GRADS],
        [raw, raw, pltpu.SemaphoreType.DMA((2,))],
        result=HBM,
    )
    return (outputs, input_grad, first_grad, second_grad)


def solution(mesh):
    return jax.shard_map(
        step,
        mesh=mesh,
        in_specs=(
            P("scene", "brick", None, None),
            P("scene", "brick", None, None),
            P(),
            P(),
            P("brick"),
            P("brick", None),
        ),
        out_specs=(P("scene", "brick", None, None), P("scene", "brick", None, None), P(), P()),
        check_vma=False,
    )
```

```python
import functools

import jax
import jax.numpy as jnp
from jax import lax
from jax.experimental import pallas as pl
from jax.experimental.pallas import tpu as pltpu
from jax.sharding import PartitionSpec as P


E = 8
C = 64
CAP = 4
f32 = jnp.float32
bf16 = jnp.bfloat16
offsets = [(a, b, c) for a in (-1, 0, 1) for b in (-1, 0, 1) for c in (-1, 0, 1)]
directions = [item for item in offsets if item != (0, 0, 0)]
number_of = {item: n for n, item in enumerate(directions)}

ROWS = CAP * 256
PLANE = CAP * 32
PACKED = 896


def row0(s, n, l):
    return s * 256 + (n // 2) * 128 + l * 16 + (n % 2) * 8


def flip(t):
    tt = t.T
    return jnp.concatenate([tt[:C], tt[C:]], axis=1)


def lane_low(shape):
    return lax.broadcasted_iota(jnp.int32, shape, 1) < C


def to_rows(x_ref, a_ref, tmp_ref, counts_ref):
    for s in range(CAP):
        occupied = jnp.where(s < counts_ref[0], 1.0, 0.0).astype(f32)
        for n in range(4):
            t = x_ref[0, s, :, n * 128 : (n + 1) * 128] * occupied
            tmp_ref[s * 4 + n] = flip(t)
            for l in range(E):
                a_ref[pl.ds(row0(s, n, l), 8), :] = tmp_ref[s * 4 + n, pl.ds(l, 8, stride=8), :]


def from_rows(a_ref, o_ref, tmp_ref):
    for s in range(CAP):
        for n in range(4):
            for l in range(E):
                tmp_ref[s * 4 + n, pl.ds(l, 8, stride=8), :] = a_ref[pl.ds(row0(s, n, l), 8), :]
            o_ref[0, s, :, n * 128 : (n + 1) * 128] = flip(tmp_ref[s * 4 + n])


def planes_out(a_ref, up_ref, down_ref):
    for s in range(CAP):
        for nh in range(2):
            base = s * 256 + nh * 128
            to = pl.ds(s * 32 + nh * 16, 16)
            up_ref[to, :] = a_ref[pl.ds(base + 7 * 16, 16), :].astype(bf16)
            down_ref[to, :] = a_ref[pl.ds(base, 16), :].astype(bf16)


def pre_kernel(
    counts_ref, x_hbm, w1_hbm, u_hbm, w2_hbm, a_ref, up_ref, down_ref, w1_ref, u_ref, w2_ref, tmp_ref, x_ref, sems
):
    pairs = ((x_hbm, x_ref), (w1_hbm, w1_ref), (w2_hbm, w2_ref), (u_hbm, u_ref))
    copies = [pltpu.make_async_copy(src, dst, sems.at[n]) for n, (src, dst) in enumerate(pairs)]
    for copy in copies:
        copy.start()
    copies[0].wait()
    to_rows(x_ref, a_ref, tmp_ref, counts_ref)
    planes_out(a_ref, up_ref, down_ref)
    for copy in copies[1:]:
        copy.wait()


def flat_weights(w_ref, o_ref, back):
    zero = jnp.zeros((C, C), f32)

    def block(a, b, c):
        k = 9 * (a + 1) + 3 * (b + 1) + (c + 1)
        return w_ref[26 - k].T if back else w_ref[k]

    blank = jnp.zeros((256, 128), bf16)
    for bi, b in enumerate((-1, 0, 1)):
        rows = pl.ds(bi * 256, 256)
        o_ref[0, rows, 128:] = blank
        o_ref[3, rows, :128] = blank
        for ci, c in enumerate((-1, 0, 1)):
            low, mid, high = (block(a, b, c) for a in (-1, 0, 1))
            left = jnp.concatenate([mid, high, zero, low], axis=0)
            right = jnp.concatenate([low, mid, high, zero], axis=0)
            joined = jnp.concatenate([left, right], axis=1).astype(bf16)
            o_ref[ci, rows, :128] = joined
            o_ref[ci + 1, rows, 128:] = joined


def prep1_kernel(w1_ref, f1_ref):
    flat_weights(w1_ref, f1_ref, False)


def prep2_kernel(counts_ref, w2_ref, x_ref, f2_ref, u_ref, tmp_ref):
    flat_weights(w2_ref, f2_ref, False)
    to_rows(x_ref, u_ref, tmp_ref, counts_ref)


def back_kernel(w_ref, b_ref):
    flat_weights(w_ref, b_ref, True)


def build(idx_ref, source, x_ref, layers, c):
    row = lax.broadcasted_iota(jnp.int32, (8, 128), 0)
    low = lane_low((8, 128))

    def one_slot(s, carry):
        def tile(a, b, n, l):
            base = s * 256 if (a, b, c) == (0, 0, 0) else idx_ref[s, number_of[a, b, c]]
            return source(base, n, l)

        def pair(b, n, l):
            full = tile(0, b, n, l)
            after = tile(0, b, n + 1, l) if n < 3 else tile(1, b, 0, l)
            before = tile(0, b, n - 1, l) if n > 0 else tile(-1, b, 3, l)
            return full, jnp.where(low, after, before)

        for nh in range(2):
            for at, l in layers:
                parts = [[] for _ in range(6)]
                for nl in range(2):
                    n = 2 * nh + nl
                    own, left, right = pair(0, n, l), pair(-1, n, l), pair(1, n, l)
                    for h in range(2):
                        parts[h].append(pltpu.roll(jnp.where(row == 7, left[h], own[h]), 1, 0))
                        parts[2 + h].append(own[h])
                        parts[4 + h].append(pltpu.roll(jnp.where(row == 0, right[h], own[h]), 7, 0))
                for q in range(6):
                    x_ref[s, nh, at, :, q * 128 : (q + 1) * 128] = jnp.concatenate(parts[q], axis=0).astype(bf16)
        return carry

    lax.fori_loop(0, CAP, one_slot, 0)


def build_center(idx_ref, a_ref, g_ref, xc_ref):
    g_ref[pl.ds(0, ROWS), :] = a_ref[...]
    g_ref[pl.ds(ROWS, 256), :] = jnp.zeros((256, 128), f32)

    def source(base, n, l):
        return g_ref[pl.ds(pl.multiple_of(base + ((n // 2) * 128 + l * 16 + (n % 2) * 8), 8), 8), :]

    build(idx_ref, source, xc_ref, [(l, l) for l in range(E)], 0)


def build_outer(idx_ref, a_ref, lo_ref, hi_ref, pool_ref, xo_ref):
    for side, (ref, layer) in enumerate(((lo_ref, 7), (hi_ref, 0))):
        for s in range(CAP):
            for nh in range(2):
                pool_ref[side, pl.ds(s * 32 + nh * 16, 16), :] = a_ref[
                    pl.ds(s * 256 + nh * 128 + layer * 16, 16), :
                ]
        pool_ref[side, pl.ds(PLANE, PLANE), :] = ref[...].astype(f32)
        pool_ref[side, pl.ds(2 * PLANE, 32), :] = jnp.zeros((32, 128), f32)

        def source(base, n, l, side=side):
            return pool_ref[side, pl.ds(pl.multiple_of(base + ((n // 2) * 16 + (n % 2) * 8), 8), 8), :]

        build(idx_ref, source, xo_ref, [(side, 0)], -1 if side == 0 else 1)


def layers_of(xc_ref, xo_ref, first, count):
    parts = []
    if first == 0:
        parts.append(xo_ref[:, :, 0:1])
    low, high = max(first, 1), min(first + count, 9)
    if high > low:
        parts.append(xc_ref[:, :, low - 1 : high - 1])
    if first + count == 10:
        parts.append(xo_ref[:, :, 1:2])
    return parts[0] if len(parts) == 1 else jnp.concatenate(parts, axis=2)


def convolve(xc_ref, xo_ref, w_ref, firsts, epilogue):
    total = None
    count = len(firsts)
    for d in range(4):
        rows = jnp.concatenate([layers_of(xc_ref, xo_ref, l + d, 1) for l in firsts], axis=2)
        term = jnp.dot(rows.reshape(128 * count, 768), w_ref[d], preferred_element_type=f32)
        total = term if total is None else total + term
    for s in range(CAP):
        for nh in range(2):
            for i, l in enumerate(firsts):
                for h in range(2):
                    at = ((s * 2 + nh) * count + i) * 16
                    epilogue(s, nh, l + h, total[at : at + 16, h * 128 : h * 128 + 128])


def convolve_ends(xc_ref, xo_ref, w_ref, epilogue):
    total = None
    for c in range(3):
        rows = jnp.concatenate([layers_of(xc_ref, xo_ref, l + c, 1) for l in (0, 7)], axis=2)
        term = jnp.dot(rows.reshape(256, 768), w_ref[c, :, :128], preferred_element_type=f32)
        total = term if total is None else total + term
    for s in range(CAP):
        for nh in range(2):
            for i, l in enumerate((0, 7)):
                at = ((s * 2 + nh) * 2 + i) * 16
                epilogue(s, nh, l, total[at : at + 16])


CENTER = (1, 3, 5)
ALL = (0, 2, 4, 6)


def full_rows(s, nh, l):
    return pl.ds(s * 256 + nh * 128 + l * 16, 16)


def center_rows(s, nh, l):
    return pl.ds((s * 2 + nh) * 96 + (l - 1) * 16, 16)


def take_center(part_ref, full_ref):
    for s in range(CAP):
        for nh in range(2):
            full_ref[pl.ds(s * 256 + nh * 128 + 16, 96), :] = part_ref[pl.ds((s * 2 + nh) * 96, 96), :]


def logistic(v):
    return 1.0 / (1.0 + jnp.exp(-v))


def first_layer(a, v):
    q = logistic(v)
    return a + v * q, q * (1.0 + v * (1.0 - q))


def second_layer(a, v, u):
    q = logistic(v)
    return a + v * q, u * (q * (1.0 + v * (1.0 - q)))


def second_back(v, u, slope):
    grad = u + v
    return grad, grad * slope


def center_kernel(formula, count, idx_ref, a_ref, w_ref, *refs):
    extra, (xc_ref, p_ref, q_ref, g_ref) = refs[:count], refs[count:]
    build_center(idx_ref, a_ref, g_ref, xc_ref)

    def epilogue(s, nh, l, v):
        full, part = full_rows(s, nh, l), center_rows(s, nh, l)
        p_ref[part, :], q_ref[part, :] = formula(v, a_ref[full, :], *[r[full, :] for r in extra])

    convolve(xc_ref, None, w_ref, CENTER, epilogue)


def outer_kernel(formula, count, send, idx_ref, a_ref, w_ref, lo_ref, hi_ref, xc_ref, pc_ref, qc_ref, *refs):
    extra, (p_ref, q_ref, up_ref, down_ref, xo_ref, pool_ref) = refs[:count], refs[count:]
    build_outer(idx_ref, a_ref, lo_ref, hi_ref, pool_ref, xo_ref)

    def epilogue(s, nh, l, v):
        full = full_rows(s, nh, l)
        p_ref[full, :], q_ref[full, :] = formula(v, a_ref[full, :], *[r[full, :] for r in extra])

    convolve_ends(xc_ref, xo_ref, w_ref, epilogue)
    planes_out((p_ref, q_ref)[send], up_ref, down_ref)
    take_center(pc_ref, p_ref)
    take_center(qc_ref, q_ref)


def last_kernel(idx_ref, a_ref, lo_ref, hi_ref, w_ref, hg_ref, o_ref, g_ref, pool_ref, xc_ref, xo_ref, r_ref, tmp_ref):
    build_center(idx_ref, a_ref, g_ref, xc_ref)
    build_outer(idx_ref, a_ref, lo_ref, hi_ref, pool_ref, xo_ref)

    def epilogue(s, nh, l, v):
        full = full_rows(s, nh, l)
        r_ref[full, :] = hg_ref[full, :] + v

    convolve(xc_ref, xo_ref, w_ref, ALL, epilogue)
    from_rows(r_ref, o_ref, tmp_ref)


def rows_kernel(r_ref, o_ref, tmp_ref):
    from_rows(r_ref, o_ref, tmp_ref)


def weight_grad(xc_ref, xo_ref, e_ref, p_ref, ready=None):
    low = lane_low((C, 128))
    errors = e_ref[...].T.astype(bf16)
    held = None
    for c in range(3):
        rows = layers_of(xc_ref, xo_ref, c, E).reshape(ROWS, 768)
        m = jnp.dot(errors, rows, preferred_element_type=f32)
        for b in range(3):
            number = 3 * c + b
            z0, z1 = m[:C, b * 256 : b * 256 + 128], m[C:, b * 256 : b * 256 + 128]
            y0, y1 = m[:C, b * 256 + 128 : (b + 1) * 256], m[C:, b * 256 + 128 : (b + 1) * 256]
            p_ref[pl.ds(number * C, C), :] = (z0 + pltpu.roll(jnp.where(low, y1, z1), C, 1)).astype(p_ref.dtype)
            if number % 2 == 0:
                held = z1 + pltpu.roll(y0, C, 1)
                if number == 8:
                    p_ref[pl.ds((9 + number // 2) * C, C), :] = jnp.where(low, held, 0.0).astype(p_ref.dtype)
            else:
                odd = pltpu.roll(z1, C, 1) + y0
                p_ref[pl.ds((9 + number // 2) * C, C), :] = jnp.where(low, held, odd).astype(p_ref.dtype)
        if ready is not None:
            ready(c)


def w2_kernel(xc_ref, xo_ref, e_ref, p_ref):
    weight_grad(xc_ref, xo_ref, e_ref, p_ref)


def w1_kernel(xc_ref, xo_ref, e_ref, second_ref, o_hbm, p_ref, sems):
    copies = [pltpu.make_async_copy(second_ref, o_hbm.at[pl.ds(PACKED, PACKED)], sems.at[4])]
    copies[0].start()

    def send(n, start, size):
        rows = pl.ds(start, size)
        copies.append(pltpu.make_async_copy(p_ref.at[rows], o_hbm.at[rows], sems.at[n]))
        copies[-1].start()

    weight_grad(xc_ref, xo_ref, e_ref, p_ref, lambda c: send(c, c * 3 * C, 3 * C))
    send(3, 9 * C, 5 * C)
    for copy in copies:
        copy.wait()


def finish_kernel(scale, r_ref, first_hbm, second_hbm, first_ref, second_ref, sems):
    copies = []

    def send(ref, hbm, start, size):
        part = pl.ds(start, size)
        copies.append(pltpu.make_async_copy(ref.at[part], hbm.at[part], sems.at[len(copies)]))
        copies[-1].start()

    for which, (ref, hbm) in enumerate(((first_ref, first_hbm), (second_ref, second_hbm))):
        for number in range(9):
            k = 3 * (number % 3) + number // 3
            t = (r_ref[pl.ds(which * PACKED + number * C, C), :].astype(f32) * scale).T
            ref[9 + k] = t[:C]
            ref[18 + k] = t[C:]
        send(ref, hbm, 9, 18)
        for number in range(0, 9, 2):
            t = (r_ref[pl.ds(which * PACKED + (9 + number // 2) * C, C), :].astype(f32) * scale).T
            ref[3 * (number % 3) + number // 3] = t[:C]
            if number < 8:
                ref[3 * ((number + 1) % 3) + (number + 1) // 3] = t[C:]
        send(ref, hbm, 0, 9)
    for copy in copies:
        copy.wait()


VMEM = pl.BlockSpec(memory_space=pltpu.VMEM)
SMEM = pl.BlockSpec(memory_space=pltpu.SMEM)
HBM = pl.BlockSpec(memory_space=pltpu.HBM)
FIELD = jax.ShapeDtypeStruct((ROWS, 128), f32)
PLANES = jax.ShapeDtypeStruct((PLANE, 128), bf16)
CENTERS = (CAP, 2, 8, 16, 768)
OUTERS = (CAP, 2, 2, 16, 768)
MIDDLE = jax.ShapeDtypeStruct((ROWS * 3 // 4, 128), f32)
GRADS = jax.ShapeDtypeStruct((27, C, C), f32)
WEIGHTS = jax.ShapeDtypeStruct((4, 768, 256), bf16)
CUBES = jax.ShapeDtypeStruct((1, CAP, C, E * E * E), f32)
OWN = pltpu.VMEM((ROWS + 256, 128), f32)
POOL = pltpu.VMEM((2, 2 * PLANE + 32, 128), f32)
TMP = pltpu.VMEM((16, C, 128), f32)


def call(kernel, scalars, arrays, outs, scratch=(), flops=0, place=VMEM, result=VMEM):
    moved = sum(x.size * x.dtype.itemsize for x in arrays) + sum(o.size * o.dtype.itemsize for o in outs)
    return pl.pallas_call(
        kernel,
        out_shape=outs,
        in_specs=[SMEM] * len(scalars) + [place] * len(arrays),
        out_specs=[result] * len(outs),
        scratch_shapes=list(scratch),
        cost_estimate=pl.CostEstimate(flops=flops, bytes_accessed=moved, transcendentals=0),
        compiler_params=pltpu.CompilerParams(vmem_limit_bytes=24 << 20),
    )(*scalars, *arrays)


def slot_table(neighbours):
    own = neighbours - lax.axis_index("brick") * CAP
    depth = jnp.array([item[2] for item in directions], jnp.int32)[None, :]
    inside = jnp.clip(own, 0, CAP - 1)
    below = jnp.where(own >= 0, inside, jnp.clip(own + 2 * CAP, CAP, 2 * CAP - 1))
    above = jnp.clip(own, 0, 2 * CAP - 1)
    present = neighbours >= 0
    middle = jnp.where(present, inside * 256, ROWS)
    outer = jnp.where(present, jnp.where(depth < 0, below, above) * 32, 2 * PLANE)
    return jnp.where(depth == 0, middle, outer).astype(jnp.int32)


def step(features, cotangent, first_kernel, second_kernel, counts, neighbours):
    bricks = lax.axis_size("brick")
    up_pairs = [(i, (i + 1) % bricks) for i in range(bricks)]
    down_pairs = [(j, i) for i, j in up_pairs]

    def exchange(up, down):
        return lax.ppermute(up, "brick", up_pairs), lax.ppermute(down, "brick", down_pairs)

    idx = slot_table(neighbours)
    centers = jax.ShapeDtypeStruct(CENTERS, bf16)
    outers = jax.ShapeDtypeStruct(OUTERS, bf16)
    packed = jax.ShapeDtypeStruct((PACKED, 128), bf16)
    raw = pltpu.VMEM((27, C, C), f32)
    cubes = pltpu.VMEM((1, CAP, C, E * E * E), f32)
    work = 2 * ROWS * 2304 * 128
    features, cotangent, first_kernel, second_kernel = [
        pltpu.with_memory_space_constraint(v, pltpu.HBM) for v in (features, cotangent, first_kernel, second_kernel)
    ]

    def layer(formula, send, field, weights, extra, between, keep=True):
        planes = between
        xc, pc, qc = call(
            functools.partial(center_kernel, formula, len(extra)),
            [idx],
            [field, weights] + extra,
            [centers, MIDDLE, MIDDLE],
            [OWN],
            work // 2,
        )
        made = call(
            functools.partial(outer_kernel, formula, len(extra), send),
            [idx],
            [field, weights, *planes, xc, pc, qc] + extra,
            [FIELD, FIELD, PLANES, PLANES] + ([outers] if keep else []),
            [POOL] if keep else [pltpu.VMEM(OUTERS, bf16), POOL],
            work // 2,
        )
        p, q, up, down = made[:4]
        return xc, made[4] if keep else None, p, q, up, down

    taps = jax.ShapeDtypeStruct((27, C, C), f32)
    inputs, up, down, first_taps, raw_upstream, second_taps = call(
        pre_kernel,
        [counts],
        [features, first_kernel, cotangent, second_kernel],
        [FIELD, PLANES, PLANES, taps, CUBES, taps],
        [TMP, cubes, pltpu.SemaphoreType.DMA((4,))],
        place=HBM,
    )
    planes = exchange(up, down)
    (f1,) = call(prep1_kernel, [], [first_taps], [WEIGHTS])
    xc1, xo1, hidden, slope1, up, down = layer(lambda v, a: first_layer(a, v), 0, inputs, f1, [], planes)
    planes = exchange(up, down)
    f2, upstream = call(prep2_kernel, [counts], [second_taps, raw_upstream], [WEIGHTS, FIELD], [TMP])
    xc2, xo2, out_rows, second_err, up, down = layer(
        lambda v, a, u: second_layer(a, v, u), 1, hidden, f2, [upstream], planes
    )
    planes = exchange(up, down)
    (b2,) = call(back_kernel, [], [second_taps], [WEIGHTS])
    (second_local,) = call(w2_kernel, [], [xc2, xo2, second_err], [packed], (), work)
    _, _, hidden_grad, first_err, up, down = layer(
        lambda v, a, u, slope: second_back(v, u, slope), 1, second_err, b2, [upstream, slope1], planes, False
    )
    lo, hi = exchange(up, down)
    (partial,) = call(
        w1_kernel,
        [],
        [xc1, xo1, first_err, second_local],
        [jax.ShapeDtypeStruct((2 * PACKED, 128), bf16)],
        [pltpu.VMEM((PACKED, 128), bf16), pltpu.SemaphoreType.DMA((5,))],
        work,
        result=HBM,
    )
    (b1,) = call(back_kernel, [], [first_taps], [WEIGHTS])
    (input_grad,) = call(
        last_kernel,
        [idx],
        [first_err, lo, hi, b1, hidden_grad],
        [CUBES],
        [OWN, POOL, pltpu.VMEM(CENTERS, bf16), pltpu.VMEM(OUTERS, bf16), pltpu.VMEM((ROWS, 128), f32), TMP],
        work,
    )
    (outputs,) = call(rows_kernel, [], [out_rows], [CUBES], [TMP])
    axes = ("brick", "scene")
    scenes = lax.axis_size("scene")
    devices = bricks * scenes
    row = 4 if bricks % 4 == 0 else 1
    near, far = row * scenes, bricks // row
    near_groups = [list(range(z * near, (z + 1) * near)) for z in range(far)]
    far_groups = [[x + row * z for z in range(far)] for x in range(row)]
    share = 2 * PACKED // near

    def near_exchange(blocks):
        return lax.all_to_all(blocks, axes, 0, 0, axis_index_groups=near_groups, tiled=True)

    def far_exchange(blocks):
        return lax.all_to_all(blocks, "brick", 0, 0, axis_index_groups=far_groups, tiled=True)

    def total_of(blocks):
        return jnp.sum(blocks.astype(f32), axis=0).astype(bf16)

    def spread(block, count):
        return jnp.broadcast_to(block[None], (count,) + block.shape)

    scattered = near_exchange(partial.reshape(near, share, 128))
    mine = total_of(scattered)
    mine = total_of(far_exchange(spread(mine, far)))
    total = near_exchange(spread(mine, near))
    scale = float((devices * CAP * E * E * E) ** -0.5)
    first_grad, second_grad = call(
        functools.partial(finish_kernel, scale),
        [],
        [total.reshape(2 * PACKED, 128)],
        [GRADS, GRADS],
        [raw, raw, pltpu.SemaphoreType.DMA((4,))],
        result=HBM,
    )
    return (outputs, input_grad, first_grad, second_grad)


def solution(mesh):
    return jax.shard_map(
        step,
        mesh=mesh,
        in_specs=(
            P("scene", "brick", None, None),
            P("scene", "brick", None, None),
            P(),
            P(),
            P("brick"),
            P("brick", None),
        ),
        out_specs=(P("scene", "brick", None, None), P("scene", "brick", None, None), P(), P()),
        check_vma=False,
    )
```
